32 devices in a mesh: dp: 16 (over z, y, core), mp: 2 (over x).
Axes of the slice: x: 2, y: 2, z: 4, core: 2. Of those that a mesh axis runs over, the one named last changes fastest.
Arguments:
- tokens: bfloat16 [4, 16, 1024, 1024], P(None, 'dp', 'mp'), may hold values from -6 to 6
- lengths: int32 [4, 16], P(None, 'dp'), may hold values from 128 to 1024, as said below
- timesteps: int32 [4, 16], P(None, 'dp'), may hold values from 0 to 999
- norm_gains: float32 [2, 1024], replicated, may hold values from 0.5 to 1.5
- time_weight: float32 [256, 2048], replicated, may hold values from -0.375 to 0.375
- qkv_weight: bfloat16 [3, 1024, 1024], P(None, None, 'mp'), may hold values from -0.1875 to 0.1875
- out_weight: bfloat16 [1024, 1024], P('mp'), may hold values from -1.5 to 1.5
- up_weight: bfloat16 [1024, 4096], P(None, 'mp'), may hold values from -0.1875 to 0.1875
- down_weight: bfloat16 [4096, 1024], P('mp'), may hold values from -0.09375 to 0.09375
- cotangent: bfloat16 [4, 16, 1024, 1024], P(None, 'dp', 'mp'), may hold values from -6 to 6
Outputs:
- output: bfloat16 [4, 16, 1024, 1024], P(None, 'dp', 'mp')
- input_grad: bfloat16 [4, 16, 1024, 1024], P(None, 'dp', 'mp')
- qkv_grad: float32 [3, 1024, 1024], P(None, 'dp', 'mp')
- out_grad: float32 [1024, 1024], P('mp', 'dp')
- up_grad: float32 [1024, 4096], P('dp', 'mp')
- down_grad: float32 [4096, 1024], P('mp', 'dp')
- gains_grad: float32 [2, 1024], P(None, ('dp', 'mp'))
- time_grad: float32 [256, 2048], P(None, ('dp', 'mp'))
The draws below stay inside these ranges and needn't reach their ends.
Inputs may be any that keep to these rules, and one draw needn't show every extreme that they name: `lengths`: in every micro-batch some sequence has all 1024 positions live.
All inputs are finite; a program needn't handle non-finite values.
Results may differ from the reference program's by a relative error of at most 0.02.
Values may be sent and summed in bfloat16 or wider, within the bound.
No kernel may reach another device: no remote copies, remote signals or barrier semaphores. Data moves between devices by JAX's collectives and lax.ppermute only.
A program may use at most 256 MiB of HBM per device.

```python
import math
import jax
import jax.numpy as jnp
from jax import lax

D = 1024
HEADS = 16
HEAD = 64
FF = 4096
TEMB = 256
LEN = 1024
MICRO = 4
SEQS = 16


def draw_lengths(key, part):
    shortest = LEN // 8
    range_size = LEN - shortest + 1
    draw_one = jax.random.randint(jax.random.fold_in(key, 11), (MICRO, SEQS), 0, range_size)
    draw_two = jax.random.randint(jax.random.fold_in(key, 12), (MICRO, SEQS), 0, range_size)
    chosen = jax.random.randint(jax.random.fold_in(key, 13), (MICRO, 1), 0, SEQS)
    seq_lengths = shortest + draw_one * draw_two // range_size
    full_len = jnp.full((MICRO, SEQS), LEN, jnp.int32)
    return jnp.where(jnp.arange(SEQS)[None, :] == chosen, full_len, seq_lengths).astype(jnp.int32)


def touch_ends(result, key, low, top_value):
    extent = result.shape
    index_at = [jax.random.randint(jax.random.fold_in(key, axis), (), 0, extent[axis]) for axis in range(len(extent))]
    result = result.at[tuple(index_at)].set(low)
    longest = extent.index(max(extent))
    index_at[longest] = (index_at[longest] + 1) % extent[longest]
    return result.at[tuple(index_at)].set(top_value)


def shard_levels(stream_key, extent, cuts, smallest, high):
    loudness, own = 1.0, jax.random.fold_in(stream_key, 6)
    for dim, blocks in cuts:
        draws = jnp.exp(jax.random.uniform(jax.random.fold_in(own, dim), (blocks,), jnp.float32, smallest / len(cuts), high / len(cuts)))
        loudness = loudness * jnp.repeat(draws, extent[dim] // blocks).reshape([-1 if axis == dim else 1 for axis in range(len(extent))])
    return loudness


def gaussian(key, shape, width, bound, split=(), kind=jnp.bfloat16):
    entries = jax.random.normal(key, shape, jnp.float32) * width
    if len(split) > 0:
        entries = shard_levels(key, shape, split, -0.22, 0.18) * entries
    return jnp.clip(entries, min=-bound, max=bound).astype(kind)


def setup_inputs(seed: int = 0) -> dict:
    keys = jax.random.split(jax.random.key(seed), 11)
    return {
        "tokens": gaussian(keys[0], (MICRO, SEQS, LEN, D), 1.0, 6.0, ((1, 16), (2, 2))),
        "lengths": draw_lengths(jax.random.fold_in(keys[10], 71), 0),
        "timesteps": touch_ends(jax.random.randint(keys[2], (MICRO, SEQS), 0, 1000), jax.random.fold_in(keys[2], 1), 0, 999).astype(jnp.int32),
        "norm_gains": jnp.clip(1.0 + 0.1 * jax.random.normal(keys[3], (2, D), jnp.float32), 0.5, 1.5),
        "time_weight": gaussian(keys[4], (TEMB, 2 * D), TEMB ** -0.5, 0.375, (), jnp.float32),
        "qkv_weight": gaussian(keys[5], (3, D, HEADS * HEAD), D ** -0.5, 0.1875, ((2, 2),)),
        "out_weight": gaussian(keys[6], (HEADS * HEAD, D), 16 ** -0.5, 1.5, ((0, 2),)),
        "up_weight": gaussian(keys[7], (D, FF), D ** -0.5, 0.1875, ((1, 2),)),
        "down_weight": gaussian(keys[8], (FF, D), FF ** -0.5, 0.09375, ((0, 2),)),
        "cotangent": gaussian(keys[9], (MICRO, SEQS, LEN, D), 1.0, 6.0, ((1, 16), (2, 2))),
    }


@jax.custom_vjp
def low(v):
    return lax.optimization_barrier(v.astype(jnp.bfloat16)).astype(jnp.float32)

@jax.custom_vjp
def low_back(v):
    return v

def low_keep(v):
    return (low(v), None)

def low_pass(kept, grad):
    return (grad,)

def back_keep(v):
    return (v, None)

def back_low(kept, grad):
    return (low(grad),)
low.defvjp(low_keep, low_pass)
low_back.defvjp(back_keep, back_low)

def sinusoid(step_ids):
    half_width = TEMB // 2
    freqs = jnp.exp(-math.log(10000.0) * jnp.arange(half_width, dtype=jnp.float32) / half_width)
    angles = step_ids.astype(jnp.float32)[:, None] * freqs[None, :]
    return jnp.concatenate([jnp.sin(angles), jnp.cos(angles)], axis=1)

def normed(values, gain, scale):
    center = values - lax.optimization_barrier(jnp.mean(values, axis=-1, keepdims=True))
    spread = lax.optimization_barrier(jnp.mean(center * center, axis=-1, keepdims=True))
    return center * lax.rsqrt(spread + 1e-05) * gain * (1.0 + scale)

def layer_block(seq_x, seq_len, seq_pair, gains_f, qkv_f, out_f, up_f, down_f):
    exact = lax.Precision.HIGHEST
    model_width = seq_x.shape[1]
    seq_count = seq_x.shape[0]
    hidden_a = low(normed(seq_x, gains_f[0], seq_pair[:model_width]))
    qkv_all = low(low_back(jnp.einsum('td,cde->cte', hidden_a, qkv_f, precision=exact)))
    queries = qkv_all[0].reshape(seq_count, HEADS, HEAD)
    key_rows = qkv_all[1].reshape(seq_count, HEADS, HEAD)
    values = qkv_all[2].reshape(seq_count, HEADS, HEAD)
    raw_scores = low_back(jnp.einsum('qhd,khd->hqk', queries, key_rows, precision=exact))
    key_valid = jnp.arange(seq_count) < seq_len
    scores = jnp.where(key_valid[None, None, :], raw_scores * 0.125, -1e+30)
    probs = low(jax.nn.softmax(scores, axis=-1))
    mixed_heads = jnp.einsum('hqk,khd->qhd', probs, values, precision=exact).reshape(seq_count, HEADS * HEAD)
    mixed_heads = low(low_back(mixed_heads))
    attn_branch = low_back(jnp.dot(mixed_heads, out_f, precision=exact))
    resid = seq_x + attn_branch
    hidden_b = low(normed(resid, gains_f[1], seq_pair[model_width:]))
    up_proj = low_back(jnp.dot(hidden_b, up_f, precision=exact))
    activated = low(jax.nn.gelu(up_proj, approximate=False))
    mlp_branch = low_back(jnp.dot(activated, down_f, precision=exact))
    return resid + mlp_branch

def reference(tokens, lengths, timesteps, norm_gains, time_weight, qkv_weight, out_weight, up_weight, down_weight, cotangent):
    model_width = tokens.shape[-1]
    seq_inputs = tokens.reshape(-1, LEN, model_width).astype(jnp.float32)
    seq_cot = cotangent.reshape(-1, LEN, model_width).astype(jnp.float32)
    seq_lengths = lengths.reshape(-1).astype(jnp.int32)
    feats = sinusoid(timesteps.reshape(-1))
    params = (norm_gains.astype(jnp.float32), time_weight.astype(jnp.float32), qkv_weight.astype(jnp.float32), out_weight.astype(jnp.float32), up_weight.astype(jnp.float32), down_weight.astype(jnp.float32))

    def forward(inputs, weights):
        gains_f, time_f, qkv_f, out_f, up_f, down_f = weights
        pairs = jnp.dot(feats, time_f, precision=lax.Precision.HIGHEST)

        def one_seq(packed):
            seq_x, seq_len, seq_pair = packed
            return layer_block(seq_x, seq_len, seq_pair, gains_f, qkv_f, out_f, up_f, down_f)
        return lax.map(jax.checkpoint(one_seq), (inputs, seq_lengths, pairs))
    outputs, pullback = jax.vjp(forward, seq_inputs, params)
    d_inputs, d_params = pullback(seq_cot)
    return (outputs.reshape(tokens.shape).astype(jnp.bfloat16), d_inputs.reshape(tokens.shape).astype(jnp.bfloat16), d_params[2], d_params[3], d_params[4], d_params[5], d_params[0], d_params[1])
```

```python
import math

import jax
import jax.numpy as jnp
from jax import lax
from jax.experimental import pallas as pl
from jax.experimental.pallas import tpu as pltpu
from jax.sharding import PartitionSpec as P

HEAD = 64
TEMB = 256


def sinusoid(step_ids):
    half_width = TEMB // 2
    freqs = jnp.exp(-math.log(10000.0) * jnp.arange(half_width, dtype=jnp.float32) / half_width)
    angles = step_ids.astype(jnp.float32)[:, None] * freqs[None, :]
    return jnp.concatenate([jnp.sin(angles), jnp.cos(angles)], axis=1)


def normed(values, gain, scale):
    center = values - jnp.mean(values, axis=-1, keepdims=True)
    spread = jnp.mean(center * center, axis=-1, keepdims=True)
    return center * lax.rsqrt(spread + 1e-05) * gain * (1.0 + scale)


def exact_gelu(values):
    return jax.nn.gelu(values, approximate=False)


def per_device(
    tokens,
    lengths,
    timesteps,
    norm_gains,
    time_weight,
    qkv_weight,
    out_weight,
    up_weight,
    down_weight,
    cotangent,
):
    micro_count, seq_dev, row_count, model_width = tokens.shape
    item_count = micro_count * seq_dev
    seq_len = row_count * lax.axis_size("mp")
    heads_dev = qkv_weight.shape[2] // HEAD
    block_rows = min(512, seq_len)
    block_count = seq_len // block_rows
    key_pos = jnp.arange(seq_len)
    feats = sinusoid(timesteps.reshape(item_count))
    pairs = jnp.dot(feats, time_weight, precision=lax.Precision.HIGHEST)
    token_items = tokens.reshape(item_count, row_count, model_width)
    cot_items = cotangent.reshape(item_count, row_count, model_width)
    len_items = lengths.reshape(item_count)

    def masked_scores(query_block, key_rows, key_valid):
        raw_scores = (
            jnp.einsum("qhd,khd->hqk", query_block, key_rows, preferred_element_type=jnp.float32)
            * 0.125
        )
        return jnp.where(key_valid[None, None, :], raw_scores, -1e30)

    def step_item(totals, packed):
        tok_rows, cot_rows, seq_length, seq_pair = packed
        scale_a = seq_pair[:model_width]
        scale_b = seq_pair[model_width:]
        key_valid = key_pos < seq_length
        inputs_f = tok_rows.astype(jnp.float32)
        norm_a = normed(inputs_f, norm_gains[0], scale_a)
        hidden_a = lax.all_gather(norm_a.astype(jnp.bfloat16), "mp", axis=0, tiled=True)
        qkv_all = jnp.einsum(
            "td,cde->cte", hidden_a, qkv_weight, preferred_element_type=jnp.float32
        ).astype(jnp.bfloat16)
        queries = qkv_all[0].reshape(seq_len, heads_dev, HEAD)
        key_rows = qkv_all[1].reshape(seq_len, heads_dev, HEAD)
        values = qkv_all[2].reshape(seq_len, heads_dev, HEAD)
        query_blocks = queries.reshape(block_count, block_rows, heads_dev, HEAD)

        def attend(query_block):
            scores = masked_scores(query_block, key_rows, key_valid)
            row_max = jnp.max(scores, axis=-1, keepdims=True)
            expo = jnp.exp(scores - row_max)
            row_sum = jnp.sum(expo, axis=-1, keepdims=True)
            probs = (expo / row_sum).astype(jnp.bfloat16)
            mixed = jnp.einsum("hqk,khd->qhd", probs, values, preferred_element_type=jnp.float32)
            return (mixed.astype(jnp.bfloat16), row_max[..., 0] + jnp.log(row_sum[..., 0]))

        mixed_blocks, log_sums = lax.map(attend, query_blocks)
        mixed_heads = mixed_blocks.reshape(seq_len, heads_dev * HEAD)
        attn_branch = lax.psum_scatter(
            jnp.dot(mixed_heads, out_weight, preferred_element_type=jnp.float32).astype(
                jnp.bfloat16
            ),
            "mp",
            scatter_dimension=0,
            tiled=True,
        ).astype(jnp.float32)
        resid = inputs_f + attn_branch
        norm_b = normed(resid, norm_gains[1], scale_b)
        hidden_b = lax.all_gather(norm_b.astype(jnp.bfloat16), "mp", axis=0, tiled=True)
        up_proj = jnp.dot(hidden_b, up_weight, preferred_element_type=jnp.float32)
        activated = exact_gelu(up_proj).astype(jnp.bfloat16)
        mlp_branch = lax.psum_scatter(
            jnp.dot(activated, down_weight, preferred_element_type=jnp.float32).astype(
                jnp.bfloat16
            ),
            "mp",
            scatter_dimension=0,
            tiled=True,
        ).astype(jnp.float32)
        layer_out = (resid + mlp_branch).astype(jnp.bfloat16)
        cot_all = lax.all_gather(cot_rows, "mp", axis=0, tiled=True)
        d_act = jnp.einsum("td,fd->tf", cot_all, down_weight, preferred_element_type=jnp.float32)
        grad_down = jnp.einsum("tf,td->fd", activated, cot_all, preferred_element_type=jnp.float32)
        gelu_out, gelu_pull = jax.vjp(exact_gelu, up_proj)
        d_up = gelu_pull(d_act)[0].astype(jnp.bfloat16)
        grad_up = jnp.einsum("td,tf->df", hidden_b, d_up, preferred_element_type=jnp.float32)
        d_norm_b = lax.psum_scatter(
            jnp.einsum("tf,df->td", d_up, up_weight, preferred_element_type=jnp.float32).astype(
                jnp.bfloat16
            ),
            "mp",
            scatter_dimension=0,
            tiled=True,
        ).astype(jnp.float32)
        norm_out_b, norm_pull_b = jax.vjp(normed, resid, norm_gains[1], scale_b)
        d_resid_ln, d_gain_b, d_scale_b = norm_pull_b(d_norm_b)
        d_resid = cot_rows.astype(jnp.float32) + d_resid_ln
        d_branch = lax.all_gather(d_resid.astype(jnp.bfloat16), "mp", axis=0, tiled=True)
        d_mixed = jnp.einsum(
            "td,ed->te", d_branch, out_weight, preferred_element_type=jnp.float32
        ).astype(jnp.bfloat16)
        grad_out = jnp.einsum(
            "te,td->ed", mixed_heads, d_branch, preferred_element_type=jnp.float32
        )
        d_mixed_blocks = d_mixed.reshape(block_count, block_rows, heads_dev, HEAD)

        def attend_back(sums, block_in):
            query_block, d_mix_block, log_block = block_in
            scores = masked_scores(query_block, key_rows, key_valid)
            probs_f = jnp.exp(scores - log_block[..., None])
            d_probs = jnp.einsum(
                "qhd,khd->hqk", d_mix_block, values, preferred_element_type=jnp.float32
            )
            inner = jnp.sum(probs_f * d_probs, axis=-1, keepdims=True)
            d_raw = (probs_f * (d_probs - inner) * 0.125).astype(jnp.bfloat16)
            d_query = jnp.einsum(
                "hqk,khd->qhd", d_raw, key_rows, preferred_element_type=jnp.float32
            )
            d_key = sums[0] + jnp.einsum(
                "hqk,qhd->khd", d_raw, query_block, preferred_element_type=jnp.float32
            )
            d_value = sums[1] + jnp.einsum(
                "hqk,qhd->khd",
                probs_f.astype(jnp.bfloat16),
                d_mix_block,
                preferred_element_type=jnp.float32,
            )
            return ((d_key, d_value), d_query)

        zero_keys = jnp.zeros((seq_len, heads_dev, HEAD), jnp.float32)
        kv_sums, d_query_blocks = lax.scan(
            attend_back, (zero_keys, zero_keys), (query_blocks, d_mixed_blocks, log_sums)
        )
        d_qkv = jnp.stack(
            [
                d_query_blocks.reshape(seq_len, heads_dev * HEAD),
                kv_sums[0].reshape(seq_len, heads_dev * HEAD),
                kv_sums[1].reshape(seq_len, heads_dev * HEAD),
            ]
        ).astype(jnp.bfloat16)
        grad_qkv = jnp.einsum("td,cte->cde", hidden_a, d_qkv, preferred_element_type=jnp.float32)
        d_norm_a = lax.psum_scatter(
            jnp.einsum("cte,cde->td", d_qkv, qkv_weight, preferred_element_type=jnp.float32).astype(
                jnp.bfloat16
            ),
            "mp",
            scatter_dimension=0,
            tiled=True,
        ).astype(jnp.float32)
        norm_out_a, norm_pull_a = jax.vjp(normed, inputs_f, norm_gains[0], scale_a)
        d_input_ln, d_gain_a, d_scale_a = norm_pull_a(d_norm_a)
        input_grad = (d_resid + d_input_ln).astype(jnp.bfloat16)
        weight_terms = (grad_qkv, grad_out, grad_up, grad_down)
        new_weights = jax.tree.map(lambda held, fresh: held + fresh, totals[0], weight_terms)
        new_gains = totals[1] + jnp.stack([d_gain_a, d_gain_b])
        d_pair = jnp.concatenate([d_scale_a, d_scale_b])
        return ((new_weights, new_gains), (layer_out, input_grad, d_pair))

    start_weights = (
        jnp.zeros(qkv_weight.shape, jnp.float32),
        jnp.zeros(out_weight.shape, jnp.float32),
        jnp.zeros(up_weight.shape, jnp.float32),
        jnp.zeros(down_weight.shape, jnp.float32),
    )
    start_gains = jnp.zeros(norm_gains.shape, jnp.float32)
    final_totals, per_item = lax.scan(
        step_item, (start_weights, start_gains), (token_items, cot_items, len_items, pairs)
    )
    weight_totals, gain_totals = final_totals
    layer_outs, input_grads, d_pairs = per_item
    weight_totals = (
        lax.psum_scatter(
            weight_totals[0].astype(jnp.bfloat16), "dp", scatter_dimension=1, tiled=True
        ).astype(jnp.float32),
        lax.psum_scatter(
            weight_totals[1].astype(jnp.bfloat16), "dp", scatter_dimension=1, tiled=True
        ).astype(jnp.float32),
        lax.psum_scatter(
            weight_totals[2].astype(jnp.bfloat16), "dp", scatter_dimension=0, tiled=True
        ).astype(jnp.float32),
        lax.psum_scatter(
            weight_totals[3].astype(jnp.bfloat16), "dp", scatter_dimension=1, tiled=True
        ).astype(jnp.float32),
    )
    time_part = jnp.dot(feats.T, d_pairs, precision=lax.Precision.HIGHEST)
    gains_grad, time_grad = (
        lax.psum_scatter(gain_totals, ("dp", "mp"), scatter_dimension=1, tiled=True),
        lax.psum_scatter(time_part, ("dp", "mp"), scatter_dimension=1, tiled=True),
    )
    return (
        layer_outs.reshape(tokens.shape),
        input_grads.reshape(tokens.shape),
        weight_totals[0],
        weight_totals[1],
        weight_totals[2],
        weight_totals[3],
        gains_grad,
        time_grad,
    )


BF = jnp.bfloat16
F32 = jnp.float32
VMEM_LIMIT = 62 << 20
EXP_SCALE = 0.125 * math.log2(math.e)
HOLD = pl.Buffered(1)
ANY = pl.BlockSpec(memory_space=pl.ANY)


def contract(left, right, left_dim, right_dim):
    return lax.dot_general(
        left, right, (((left_dim,), (right_dim,)), ((), ())), preferred_element_type=F32
    )


def call(body, meta, args, grid, in_specs, out_specs, out_shape, flops, scratch=(), aliases=None):
    moved = sum(a.size * a.dtype.itemsize for a in args)
    moved += sum(math.prod(o.shape) * jnp.dtype(o.dtype).itemsize for o in out_shape)
    return pl.pallas_call(
        body,
        grid_spec=pltpu.PrefetchScalarGridSpec(
            num_scalar_prefetch=1,
            grid=grid,
            in_specs=in_specs,
            out_specs=out_specs,
            scratch_shapes=list(scratch),
        ),
        out_shape=out_shape,
        input_output_aliases=aliases or {},
        compiler_params=pltpu.CompilerParams(vmem_limit_bytes=VMEM_LIMIT),
        cost_estimate=pl.CostEstimate(flops=int(flops), bytes_accessed=int(moved), transcendentals=0),
    )(meta, *args)


def shape(dims, kind=BF):
    return jax.ShapeDtypeStruct(tuple(dims), kind)


def normalize(values):
    center = values - jnp.mean(values, axis=-1, keepdims=True)
    spread = jnp.mean(center * center, axis=-1, keepdims=True)
    root = lax.rsqrt(spread + 1e-05)
    return center * root, root


def norm_back(d_out, unit, root, gain):
    d_unit = d_out * gain
    return root * (
        d_unit
        - jnp.mean(d_unit, axis=-1, keepdims=True)
        - unit * jnp.mean(d_unit * unit, axis=-1, keepdims=True)
    )


def first_proj(meta, s, tok, recv, gain, weight, prev):
    _, rows, width = tok.shape
    part = weight.shape[2]
    seqs = gain.shape[0]

    def body(m, loc, rec, g, w, *refs):
        tokf, hid, qkv = refs[-3:]

        @pl.when(pl.program_id(0) == m[0])
        def _():
            tokf[0] = loc[0]

        @pl.when(pl.program_id(0) != m[0])
        def _():
            tokf[0] = rec[0]

        unit, _ = normalize(tokf[0].astype(F32))
        hidden = (unit * g[0]).astype(BF)
        hid[0] = hidden
        for c in range(3):
            qkv[0, c] = contract(w[c], hidden, 0, 1).astype(BF)

    length = 2 * rows
    outs = [shape((seqs, length, width)), shape((seqs, length, width)), shape((seqs, 3, part, length))]
    return call(
        body,
        meta,
        [tok, recv, gain, weight] + list(prev),
        (2,),
        [
            pl.BlockSpec((1, rows, width), lambda h, m: (m[1 + s], 0, 0)),
            pl.BlockSpec((1, rows, width), lambda h, m: (0, 0, 0)),
            pl.BlockSpec((1, 1, width), lambda h, m: (s, 0, 0)),
            pl.BlockSpec((3, width, part), lambda h, m: (0, 0, 0), pipeline_mode=HOLD),
        ]
        + [ANY] * len(prev),
        [
            pl.BlockSpec((1, rows, width), lambda h, m: (s, h, 0)),
            pl.BlockSpec((1, rows, width), lambda h, m: (s, h, 0)),
            pl.BlockSpec((1, 3, part, rows), lambda h, m: (s, 0, 0, h)),
        ],
        outs,
        6 * length * width * part,
        aliases={5 + i: i for i in range(len(prev))},
    )


def other_proj(meta, hid, weight, s, prev):
    seqs, length, width = hid.shape
    part = weight.shape[2]
    rows = length // 2

    def body(m, h_ref, w, *refs):
        for c in range(3):
            refs[-1][0, c] = contract(w[c], h_ref[0], 0, 1).astype(BF)

    return call(
        body,
        meta,
        [hid, weight] + list(prev),
        (2,),
        [
            pl.BlockSpec((1, rows, width), lambda h, m: (s, h, 0)),
            pl.BlockSpec((3, width, part), lambda h, m: (0, 0, 0), pipeline_mode=HOLD),
        ]
        + [ANY] * len(prev),
        [pl.BlockSpec((1, 3, part, rows), lambda h, m: (s, 0, 0, h))],
        [shape((seqs, 3, part, length))],
        6 * length * width * part,
        aliases={3 + i: i for i in range(len(prev))},
    )


def mask_rows(valid, length, block):
    first = lax.broadcasted_iota(jnp.int32, (16, length), 0) == 0
    hidden = lax.broadcasted_iota(jnp.int32, (16, length), 1) >= valid
    keys = jnp.where(first & hidden, -1e30, 0.0).astype(BF)
    ones = jnp.where(lax.broadcasted_iota(jnp.int32, (16, block), 0) == 0, 1.0, 0.0).astype(BF)
    return keys, ones


def attention(meta, qkv, first, count, prev):
    seqs, _, part, length = qkv.shape
    heads = part // HEAD
    view = qkv.reshape(seqs, 3, heads, HEAD, length)
    lens_at = 1 + seqs

    def body(m, q, k, v, *refs):
        out, logs = refs[-2:]
        valid = m[lens_at + first + pl.program_id(0)]
        key_mask, ones = mask_rows(valid, length, length)
        scores = contract(
            jnp.concatenate([k[0, 0, 0], key_mask], 0), jnp.concatenate([q[0, 0, 0], ones], 0), 0, 0
        )
        top = jnp.max(scores, 0, keepdims=True)
        expo = jnp.exp2((scores - top) * EXP_SCALE)
        total = jnp.sum(expo, 0, keepdims=True)
        mixed = contract(v[0, 0, 0], expo.astype(BF), 1, 0)
        out[0, 0] = (mixed / total).astype(BF)
        logs[0, 0] = top * EXP_SCALE + jnp.log2(total)

    def spec(c):
        return pl.BlockSpec((1, 1, 1, HEAD, length), lambda s, h, m: (s + first, c, h, 0, 0))

    return call(
        body,
        meta,
        [view, view, view] + list(prev),
        (count, heads),
        [spec(0), spec(1), spec(2)] + [ANY] * len(prev),
        [
            pl.BlockSpec((1, 1, HEAD, length), lambda s, h, m: (s + first, h, 0, 0)),
            pl.BlockSpec((1, 1, 1, length), lambda s, h, m: (s + first, h, 0, 0)),
        ],
        [shape((seqs, heads, HEAD, length)), shape((seqs, heads, 1, length), F32)],
        16 * count * heads * length * length * HEAD,
        aliases={4 + i: i for i in range(len(prev))},
    )


def attention_back(meta, qkv, out, d_out, logs, first, prev):
    seqs, _, part, length = qkv.shape
    heads = part // HEAD
    view = qkv.reshape(seqs, 3, heads, HEAD, length)
    lens_at = 1 + seqs
    block = min(256, length)
    group = 2 if heads % 2 == 0 else 1

    def body(m, q, k, v, o, do, ls, *refs):
        d_qkv, dk_sum, dv_sum = refs[-3:]
        valid = m[lens_at + first]
        key_mask, ones = mask_rows(valid, length, block)
        for h in range(group):
            keys = k[0, 0, h]
            masked_keys = jnp.concatenate([keys, key_mask], 0)
            for i in range(length // block):
                sl = slice(i * block, (i + 1) * block)
                query = q[0, 0, h, :, sl]
                d_mix = do[0, h, :, sl]
                scores = contract(masked_keys, jnp.concatenate([query, ones], 0), 0, 0)
                probs = jnp.exp2(scores * EXP_SCALE - ls[0, h, :, sl])
                inner = jnp.sum(d_mix.astype(F32) * o[0, h, :, sl].astype(F32), 0, keepdims=True)
                d_probs = contract(v[0, 0, h], d_mix, 0, 0)
                d_raw = (probs * (d_probs - inner) * 0.125).astype(BF)
                d_value = contract(d_mix, probs.astype(BF), 1, 1)
                d_key = contract(query, d_raw, 1, 1)
                if i == 0:
                    dk_sum[...] = d_key
                    dv_sum[...] = d_value
                else:
                    dk_sum[...] += d_key
                    dv_sum[...] += d_value
                d_qkv[0, 0, h, :, sl] = contract(keys, d_raw, 1, 0).astype(BF)
            d_qkv[0, 1, h] = dk_sum[...].astype(BF)
            d_qkv[0, 2, h] = dv_sum[...].astype(BF)

    def spec(c):
        return pl.BlockSpec((1, 1, group, HEAD, length), lambda h, m: (first, c, h, 0, 0))

    head_spec = pl.BlockSpec((1, group, HEAD, length), lambda h, m: (first, h, 0, 0))
    return call(
        body,
        meta,
        [view, view, view, out, d_out, logs] + list(prev),
        (heads // group,),
        [
            spec(0),
            spec(1),
            spec(2),
            head_spec,
            head_spec,
            pl.BlockSpec((1, group, 1, length), lambda h, m: (first, h, 0, 0)),
        ]
        + [ANY] * len(prev),
        [pl.BlockSpec((1, 3, group, HEAD, length), lambda h, m: (first, 0, h, 0, 0))],
        [shape((seqs, 3, heads, HEAD, length))],
        40 * heads * length * length * HEAD,
        scratch=[pltpu.VMEM((HEAD, length), F32)] * 2,
        aliases={7 + i: i for i in range(len(prev))},
    )


def out_proj(meta, own_mix, oth_mix, tokf, cot, cot_recv, own_w, oth_w, gain):
    seqs, length, width = tokf.shape
    rows = length // 2
    part = own_w.shape[0]
    own_mix = own_mix.reshape(seqs, part, length)
    oth_mix = oth_mix.reshape(seqs, part, length)

    def body(m, a, b, t, cl, cr, wa, wb, g, resid, hid, cotf):
        @pl.when(pl.program_id(1) == m[0])
        def _():
            cotf[0] = cl[0]

        @pl.when(pl.program_id(1) != m[0])
        def _():
            cotf[0] = cr[0]

        branch = contract(a[0], wa[...], 0, 0) + contract(b[0], wb[...], 0, 0)
        total = t[0].astype(F32) + branch
        resid[0] = total.astype(BF)
        unit, _ = normalize(total)
        hid[0] = (unit * g[0]).astype(BF)

    mix_spec = pl.BlockSpec((1, part, rows), lambda s, h, m: (s, 0, h))
    row_spec = pl.BlockSpec((1, rows, width), lambda s, h, m: (s, h, 0))
    w_spec = pl.BlockSpec((part, width), lambda s, h, m: (0, 0), pipeline_mode=HOLD)
    return call(
        body,
        meta,
        [own_mix, oth_mix, tokf, cot, cot_recv, own_w, oth_w, gain],
        (seqs, 2),
        [
            mix_spec,
            mix_spec,
            row_spec,
            pl.BlockSpec((1, rows, width), lambda s, h, m: (m[1 + s], 0, 0)),
            pl.BlockSpec((1, rows, width), lambda s, h, m: (s, 0, 0)),
            w_spec,
            w_spec,
            pl.BlockSpec((1, 1, width), lambda s, h, m: (s, 0, 0)),
        ],
        [row_spec] * 3,
        [shape((seqs, length, width))] * 3,
        4 * seqs * length * width * part,
    )


def feed_forward(meta, hid, cot, up_w, down_w, sums):
    seqs, length, width = hid.shape
    tokens = seqs * length
    hidden = up_w.shape[1]
    block = min(512, hidden)
    rows = min(512, tokens)
    steps = hidden // block
    last = len(sums) > 0
    half_root = 1.0 / math.sqrt(2.0)
    density = 1.0 / math.sqrt(2.0 * math.pi)

    def body(m, h_ref, c_ref, wu, wd, *refs):
        sums_in = refs[: len(sums)]
        out, d_hid, grads, act, d_up, out_sum, hid_sum, stage, sem = refs[len(sums) :]
        step = pl.program_id(0)

        def moves(r):
            sl = pl.ds(r * rows, rows)
            if last:
                return [
                    pltpu.make_async_copy(sums_in[0].at[sl], out_sum.at[sl], sem.at[0, r]),
                    pltpu.make_async_copy(sums_in[1].at[sl], hid_sum.at[sl], sem.at[1, r]),
                ]
            return [
                pltpu.make_async_copy(out_sum.at[sl], out.at[sl], sem.at[0, r]),
                pltpu.make_async_copy(hid_sum.at[sl], d_hid.at[sl], sem.at[1, r]),
            ]

        def stores(r):
            sl = pl.ds(r * rows, rows)
            return [
                pltpu.make_async_copy(stage.at[0, r], out.at[sl], sem.at[0, r]),
                pltpu.make_async_copy(stage.at[1, r], d_hid.at[sl], sem.at[1, r]),
            ]

        count = tokens // rows

        @pl.when(step == 0)
        def _():
            if last:
                for r in range(count):
                    for move in moves(r):
                        move.start()
            else:
                out_sum[...] = jnp.zeros_like(out_sum)
                hid_sum[...] = jnp.zeros_like(hid_sum)

        for r in range(count):
            sl = slice(r * rows, (r + 1) * rows)
            up = contract(h_ref[sl, :], wu[...], 1, 0)
            d_act = contract(c_ref[sl, :], wd[...], 1, 1)
            cdf = 0.5 * (1.0 + lax.erf(up * half_root))
            slope = cdf + up * (density * jnp.exp(-0.5 * up * up))
            a = (up * cdf).astype(BF)
            d = (d_act * slope).astype(BF)
            act[sl, :] = a
            d_up[sl, :] = d
            if last:

                @pl.when(step == 0)
                def _():
                    for move in moves(r):
                        move.wait()

            out_sum[sl, :] += contract(a, wd[...], 1, 0)
            hid_sum[sl, :] += contract(d, wu[...], 1, 1)

            @pl.when(step == steps - 1)
            def _():
                if last:
                    stage[0, r] = out_sum[sl, :].astype(BF)
                    stage[1, r] = hid_sum[sl, :].astype(BF)
                for move in stores(r) if last else moves(r):
                    move.start()

        grads[0] = contract(h_ref[...], d_up[...], 0, 0).astype(BF)
        grads[1] = contract(c_ref[...], act[...], 0, 0).astype(BF)

        @pl.when(step == steps - 1)
        def _():
            for r in range(count):
                for move in stores(r) if last else moves(r):
                    move.wait()

    kind = BF if last else F32
    full = pl.BlockSpec((tokens, width), lambda j, m: (0, 0), pipeline_mode=HOLD)
    staged = (2, tokens // rows, rows, width) if last else (1, 1, 16, 128)
    return call(
        body,
        meta,
        [hid.reshape(tokens, width), cot.reshape(tokens, width), up_w, down_w] + list(sums),
        (steps,),
        [
            full,
            full,
            pl.BlockSpec((width, block), lambda j, m: (0, j)),
            pl.BlockSpec((block, width), lambda j, m: (j, 0)),
        ]
        + [ANY] * len(sums),
        [ANY, ANY, pl.BlockSpec((2, width, block), lambda j, m: (0, 0, j))],
        [shape((tokens, width), kind), shape((tokens, width), kind), shape((2, width, hidden))],
        12 * tokens * width * hidden,
        scratch=[
            pltpu.VMEM((tokens, block), BF),
            pltpu.VMEM((tokens, block), BF),
            pltpu.VMEM((tokens, width), F32),
            pltpu.VMEM((tokens, width), F32),
            pltpu.VMEM(staged, BF),
            pltpu.SemaphoreType.DMA((2, tokens // rows)),
        ],
    )


def middle(meta, resid, mlp, d_hid, cotf, own_mix, oth_mix, own_w, oth_w, gain, items):
    seqs, length, width = resid.shape
    rows = length // 2
    part = own_w.shape[0]
    mixes = [a.reshape(seqs, part, length) for a in (own_mix, oth_mix)]
    mlp = mlp.reshape(resid.shape)
    d_hid = d_hid.reshape(resid.shape)

    def body(m, res, up, dh, ct, ma, mb, wa, wb, g, mine, away, branch, dma, dmb, grad, gsum, grad_sum, vec):
        phase, s = pl.program_id(0), pl.program_id(1)

        @pl.when((phase == 0) & (s == 0))
        def _():
            grad_sum[...] = jnp.zeros_like(grad_sum)
            vec[...] = jnp.zeros_like(vec)

        resid_f = res[0].astype(F32)
        total = (resid_f + up[0].astype(F32)).astype(BF)

        @pl.when(phase == 0)
        def _():
            away[0] = total

        @pl.when(phase == 1)
        def _():
            mine[0] = total

        unit, root = normalize(resid_f)
        d_out = dh[0].astype(F32)
        vec[s] += jnp.sum(d_out * unit, axis=0, keepdims=True)
        d_res = (ct[0].astype(F32) + norm_back(d_out, unit, root, g[0])).astype(BF)
        branch[0] = d_res
        dma[0] = contract(wa[...], d_res, 1, 1).astype(BF)
        dmb[0] = contract(wb[...], d_res, 1, 1).astype(BF)
        grad_sum[0] += contract(d_res, ma[0], 0, 1)
        grad_sum[1] += contract(d_res, mb[0], 0, 1)

        @pl.when((phase == 1) & (s == seqs - 1))
        def _():
            grad[...] = grad_sum[...].astype(BF)
            gsum[...] = vec[...]

    def at(p, m):
        return (1 - m[0]) + p * (2 * m[0] - 1)

    row_spec = pl.BlockSpec((1, rows, width), lambda p, s, m: (s, at(p, m), 0))
    mix_spec = pl.BlockSpec((1, part, rows), lambda p, s, m: (s, 0, at(p, m)))
    w_spec = pl.BlockSpec((part, width), lambda p, s, m: (0, 0), pipeline_mode=HOLD)
    return call(
        body,
        meta,
        [resid, mlp, d_hid, cotf, mixes[0], mixes[1], own_w, oth_w, gain],
        (2, seqs),
        [row_spec] * 4
        + [mix_spec] * 2
        + [w_spec] * 2
        + [pl.BlockSpec((1, 1, width), lambda p, s, m: (s, 0, 0))],
        [
            pl.BlockSpec((1, rows, width), lambda p, s, m: (m[1 + p * s], 0, 0)),
            pl.BlockSpec((1, rows, width), lambda p, s, m: (s + p * (seqs - 1 - s), 0, 0)),
            row_spec,
            mix_spec,
            mix_spec,
            pl.BlockSpec((2, width, part), lambda p, s, m: (0, 0, 0), pipeline_mode=HOLD),
            pl.BlockSpec((seqs, 1, width), lambda p, s, m: (0, 0, 0)),
        ],
        [
            shape((items, rows, width)),
            shape((seqs, rows, width)),
            shape((seqs, length, width)),
            shape((seqs, part, length)),
            shape((seqs, part, length)),
            shape((2, width, part)),
            shape((seqs, 1, width), F32),
        ],
        8 * seqs * length * width * part,
        scratch=[pltpu.VMEM((2, width, part), F32), pltpu.VMEM((seqs, 1, width), F32)],
    )


def proj_grad(meta, hid, d_qkv):
    seqs, length, width = hid.shape
    part = d_qkv.shape[2] * d_qkv.shape[3]
    d_qkv = d_qkv.reshape(seqs, 3, part, length)

    def body(m, h_ref, d_ref, grad):
        total = contract(d_ref[0, 0], h_ref[0], 1, 0)
        for s in range(1, seqs):
            total += contract(d_ref[s, 0], h_ref[s], 1, 0)
        grad[0] = total.astype(BF).T

    return call(
        body,
        meta,
        [hid, d_qkv],
        (3,),
        [
            pl.BlockSpec((seqs, length, width), lambda c, m: (0, 0, 0), pipeline_mode=HOLD),
            pl.BlockSpec((seqs, 1, part, length), lambda c, m: (0, c, 0, 0)),
        ],
        [pl.BlockSpec((1, width, part), lambda c, m: (c, 0, 0))],
        [shape((3, width, part))],
        6 * seqs * length * width * part,
    )[0]


def input_back(meta, tokf, branch, own_d, oth_d, own_w, oth_w, gain, items, stay, first, count):
    seqs, length, width = tokf.shape
    rows = length // 2
    part = own_w.shape[2]
    own_d = own_d.reshape(seqs, 3, part, length)
    oth_d = oth_d.reshape(seqs, 3, part, length)

    def body(m, tok, br, da, db, wa, wb, g, out, gsum):
        d_hid = contract(da[0, 0], wa[0], 0, 1) + contract(db[0, 0], wb[0], 0, 1)
        for c in range(1, 3):
            d_hid += contract(da[0, c], wa[c], 0, 1) + contract(db[0, c], wb[c], 0, 1)
        unit, root = normalize(tok[0].astype(F32))
        gsum[0] = jnp.sum(d_hid * unit, axis=0, keepdims=True)
        out[0] = (br[0].astype(F32) + norm_back(d_hid, unit, root, g[0])).astype(BF)

    def at(m):
        return m[0] if stay else 1 - m[0]

    row_spec = pl.BlockSpec((1, rows, width), lambda s, m: (s + first, at(m), 0))
    d_spec = pl.BlockSpec((1, 3, part, rows), lambda s, m: (s + first, 0, 0, at(m)))
    w_spec = pl.BlockSpec((3, width, part), lambda s, m: (0, 0, 0), pipeline_mode=HOLD)
    return call(
        body,
        meta,
        [tokf, branch, own_d, oth_d, own_w, oth_w, gain],
        (count,),
        [row_spec, row_spec, d_spec, d_spec, w_spec, w_spec]
        + [pl.BlockSpec((1, 1, width), lambda s, m: (s + first, 0, 0))],
        [
            pl.BlockSpec((1, rows, width), lambda s, m: (m[1 + s] if stay else s, 0, 0)),
            pl.BlockSpec((1, 1, width), lambda s, m: (s, 0, 0)),
        ],
        [shape((items if stay else count, rows, width)), shape((count, 1, width), F32)],
        12 * count * rows * width * part,
    )


def place(meta, base, came, first, seqs):
    count, rows, width = came.shape
    at = 1 + 2 * seqs + first

    def body(m, src, _, out):
        out[...] = src[...]

    return call(
        body,
        meta,
        [came, base],
        (count,),
        [pl.BlockSpec((1, rows, width), lambda s, m: (s, 0, 0)), ANY],
        [pl.BlockSpec((1, rows, width), lambda s, m: (m[at + s], 0, 0))],
        [shape(base.shape)],
        1,
        aliases={2: 0},
    )[0]


def after(value, *earlier):
    return lax.optimization_barrier((value,) + earlier)[0]


def per_device_pair(
    tokens,
    lengths,
    timesteps,
    norm_gains,
    time_weight,
    qkv_weight,
    out_weight,
    up_weight,
    down_weight,
    cotangent,
):
    micro_count, seq_dev, rows, width = tokens.shape
    items = micro_count * seq_dev
    seqs = items // 2
    x = lax.axis_index("mp")
    dp = lax.axis_index("dp")
    dp_count = lax.axis_size("dp")
    part = qkv_weight.shape[2]
    hidden = up_weight.shape[1]
    tok = tokens.reshape(items, rows, width)
    cot = cotangent.reshape(items, rows, width)
    lens = lengths.reshape(items)
    own = x * seqs + jnp.arange(seqs, dtype=jnp.int32)
    oth = (1 - x) * seqs + jnp.arange(seqs, dtype=jnp.int32)
    meta = jnp.concatenate([x[None].astype(jnp.int32), own, lens[own], oth]).astype(jnp.int32)
    steps = timesteps.reshape(items)

    def swap(value):
        return lax.ppermute(value, "mp", [(0, 1), (1, 0)])

    def shard(value):
        count = value.shape[0] // dp_count
        return lax.dynamic_slice_in_dim(value, dp * count, count, 0)

    def spread(value):
        return lax.all_gather(value, "dp", axis=0, tiled=True)

    qkv_rows = qkv_weight.reshape(3 * width, part)
    qkv_shard = swap(shard(qkv_rows))
    qkv_oth = spread(qkv_shard).reshape(qkv_weight.shape)
    def sent(rows_of, s, count):
        return lax.dynamic_slice_in_dim(rows_of, (1 - x) * seqs + s, count, 0)

    tok_recv = [swap(sent(tok, 0, 1))]

    feats = sinusoid(lax.dynamic_slice_in_dim(steps, x * seqs, seqs, 0))
    pairs = jnp.dot(feats, time_weight, precision=lax.Precision.HIGHEST)
    widened = 1.0 + pairs.reshape(seqs, 2, 1, width)
    gain_a = norm_gains[0] * widened[:, 0]
    gain_b = norm_gains[1] * widened[:, 1]

    far_shards = [swap(after(shard(w), tok_recv[0])) for w in (out_weight, up_weight, down_weight)]
    base, qkv_far, mix_own, mix_oth = (), (), (), ()
    for s in range(seqs):
        base = first_proj(meta, s, tok, tok_recv[s], gain_a, qkv_weight, base)
        mix_own = attention(meta, base[2], s, 1, mix_own)
        if s == 0:
            out_oth, up_oth, down_oth = [spread(after(w, mix_own[1])) for w in far_shards]
        if s + 1 < seqs:
            tok_recv.append(swap(after(sent(tok, s + 1, 1), mix_own[1], *far_shards)))
        qkv_far = other_proj(meta, base[1], qkv_oth, s, qkv_far)
        mix_oth = attention(meta, qkv_far[0], s, 1, mix_oth)
        if s == 0:
            cot_recv = swap(after(sent(cot, 0, seqs), mix_oth[1], tok_recv[-1]))
    tokf, hid_a, qkv_own = base
    qkv_far = qkv_far[0]
    resid, hid_b, cotf = out_proj(
        meta, mix_own[0], mix_oth[0], tokf, cot, cot_recv, out_weight, out_oth, gain_b
    )
    out_part, hid_part, grads_own = feed_forward(meta, hid_b, cotf, up_weight, down_weight, ())
    mlp, d_hid_b, grads_oth = feed_forward(meta, hid_b, cotf, up_oth, down_oth, (out_part, hid_part))

    def tree_send(value, step):
        count, cols = value.shape[0], value.shape[-1]
        value = value.reshape(count, -1, 1, 2, width // dp_count, cols)
        mine_at = dp // step % 2
        keep = lax.dynamic_index_in_dim(value, mine_at, 3, False)
        send = lax.dynamic_index_in_dim(value, 1 - mine_at, 3, False)
        return keep, lax.ppermute(send, "dp", [(i, i ^ step) for i in range(dp_count)])

    def tree_add(pair, gate):
        keep, came = pair[0], after(pair[1], *gate)
        return (keep.astype(F32) + came.astype(F32)).astype(BF)

    def tree(value):
        step = 1
        while step < dp_count:
            pair = tree_send(value, step)
            value = tree_add(pair, (yield value))
            step *= 2
        yield value.reshape(value.shape[0], width // dp_count, value.shape[-1])

    def reduce(value):
        return lax.psum_scatter(value, "dp", scatter_dimension=1, tiled=True)

    ffn_own = reduce(grads_own)
    ffn_oth = reduce(grads_oth)
    out_stay, out_away, branch, d_mix_own, d_mix_oth, out_grads, sum_b = middle(
        meta, resid, mlp, d_hid_b, cotf, mix_own[0], mix_oth[0], out_weight, out_oth, gain_b, items
    )
    out_came = swap(out_away)

    def heads_view(value):
        return value.reshape(seqs, part // HEAD, HEAD, 2 * rows)

    class Job:
        def __init__(self, value):
            self.run, self.value, self.done = tree(value), None, False
            self.value = next(self.run)

        def go(self, *gate):
            if not self.done:
                try:
                    self.value = self.run.send(gate)
                except StopIteration:
                    self.done = True
            return self.value

    d_mix_own, d_mix_oth = heads_view(d_mix_own), heads_view(d_mix_oth)
    jobs = [Job(out_grads)]
    d_oth, d_own = (), ()
    order = meta

    def ready(*gate):
        return after(meta, *[job.go(*gate) for job in jobs])

    for s in range(seqs):
        d_oth = attention_back(order, qkv_far, mix_oth[0], d_mix_oth, mix_oth[1], s, d_oth)
        order = ready(d_oth[0])
    grad_oth = proj_grad(order, hid_a, d_oth[0])
    jobs.append(Job(grad_oth))
    order = after(meta, grad_oth, ffn_own)
    for s in range(seqs):
        d_own = attention_back(order, qkv_own, mix_own[0], d_mix_own, mix_own[1], s, d_own)
        order = ready(d_own[0])
    grad_own = proj_grad(order, hid_a, d_own[0])
    order = ready(grad_own)
    jobs.append(Job(grad_own))
    in_away, sums_a = [], []
    for s in range(seqs):
        rows_out, vec = input_back(
            order, tokf, branch, d_own[0], d_oth[0], qkv_weight, qkv_oth, gain_a, items, False, s, 1
        )
        in_away.append(swap(rows_out))
        sums_a.append(vec)
        order = ready(rows_out)
    in_stay, sum_stay = input_back(
        after(order, ffn_oth), tokf, branch, d_own[0], d_oth[0], qkv_weight, qkv_oth, gain_a, items, True, 0, seqs
    )
    sum_a = jnp.concatenate(sums_a, 0) + sum_stay
    for job in jobs:
        while not job.done:
            job.go(in_stay)
    out_red, qkv_red_oth, qkv_red_own = [job.value for job in jobs]
    output = place(meta, out_stay, out_came, 0, seqs)
    input_grad = in_stay
    for s in range(seqs):
        input_grad = place(meta, input_grad, in_away[s], s, seqs)

    ffn = ffn_own.astype(F32) + swap(ffn_oth).astype(F32)
    out_sum = out_red[0].astype(F32) + swap(out_red[1]).astype(F32)
    qkv_sum = qkv_red_own.astype(F32) + swap(qkv_red_oth).astype(F32)

    sums = jnp.stack([sum_a, sum_b], 0)[:, :, 0]
    d_pair = sums * norm_gains[:, None, :]
    gain_part = jnp.sum(sums * jnp.swapaxes(widened[:, :, 0], 0, 1), axis=1)
    count = 2 * dp_count
    cols, gain_cols, time_cols = 2 * width // count, width // count, feats.shape[1]
    by_pair = jnp.moveaxis(d_pair.reshape(2, seqs, dp_count, cols), 1, 2).reshape(count, seqs * cols)
    by_gain = jnp.moveaxis(gain_part.reshape(2, count, gain_cols), 0, 1).reshape(count, 2 * gain_cols)
    by_feat = jnp.broadcast_to(feats.reshape(1, seqs * time_cols), (count, seqs * time_cols))
    packed = jnp.concatenate([by_pair, by_gain, by_feat], 1)
    everyone = lax.all_to_all(packed, ("dp", "mp"), 0, 0, tiled=True)
    mine = everyone[:, : seqs * cols].reshape(count * seqs, cols)
    gains_grad = jnp.sum(everyone[:, seqs * cols :][:, : 2 * gain_cols], axis=0).reshape(2, gain_cols)
    all_feats = everyone[:, seqs * cols + 2 * gain_cols :].reshape(count * seqs, time_cols)
    time_grad = jnp.dot(all_feats.T, mine, precision=lax.Precision.HIGHEST)
    return (
        output.reshape(tokens.shape),
        input_grad.reshape(tokens.shape),
        qkv_sum,
        out_sum.T,
        ffn[0],
        ffn[1].T,
        gains_grad,
        time_grad,
    )


def solution(mesh):
    in_specs = (
        P(None, "dp", "mp", None),
        P(None, "dp"),
        P(None, "dp"),
        P(),
        P(),
        P(None, None, "mp"),
        P("mp", None),
        P(None, "mp"),
        P("mp", None),
        P(None, "dp", "mp", None),
    )
    out_specs = (
        P(None, "dp", "mp", None),
        P(None, "dp", "mp", None),
        P(None, "dp", "mp"),
        P("mp", "dp"),
        P("dp", "mp"),
        P("mp", "dp"),
        P(None, ("dp", "mp")),
        P(None, ("dp", "mp")),
    )
    dp_count = mesh.shape["dp"]
    paired = mesh.shape["mp"] == 2 and dp_count & (dp_count - 1) == 0
    return jax.shard_map(
        per_device_pair if paired else per_device, mesh=mesh, in_specs=in_specs, out_specs=out_specs, check_vma=False
    )
```

```python
import math

import jax
import jax.numpy as jnp
from jax import lax
from jax.experimental import pallas as pl
from jax.experimental.pallas import tpu as pltpu
from jax.sharding import PartitionSpec as P

HEAD = 64
TEMB = 256


def sinusoid(step_ids):
    half_width = TEMB // 2
    freqs = jnp.exp(-math.log(10000.0) * jnp.arange(half_width, dtype=jnp.float32) / half_width)
    angles = step_ids.astype(jnp.float32)[:, None] * freqs[None, :]
    return jnp.concatenate([jnp.sin(angles), jnp.cos(angles)], axis=1)


def normed(values, gain, scale):
    center = values - jnp.mean(values, axis=-1, keepdims=True)
    spread = jnp.mean(center * center, axis=-1, keepdims=True)
    return center * lax.rsqrt(spread + 1e-05) * gain * (1.0 + scale)


def exact_gelu(values):
    return jax.nn.gelu(values, approximate=False)


def per_device(
    tokens,
    lengths,
    timesteps,
    norm_gains,
    time_weight,
    qkv_weight,
    out_weight,
    up_weight,
    down_weight,
    cotangent,
):
    micro_count, seq_dev, row_count, model_width = tokens.shape
    item_count = micro_count * seq_dev
    seq_len = row_count * lax.axis_size("mp")
    heads_dev = qkv_weight.shape[2] // HEAD
    block_rows = min(512, seq_len)
    block_count = seq_len // block_rows
    key_pos = jnp.arange(seq_len)
    feats = sinusoid(timesteps.reshape(item_count))
    pairs = jnp.dot(feats, time_weight, precision=lax.Precision.HIGHEST)
    token_items = tokens.reshape(item_count, row_count, model_width)
    cot_items = cotangent.reshape(item_count, row_count, model_width)
    len_items = lengths.reshape(item_count)

    def masked_scores(query_block, key_rows, key_valid):
        raw_scores = (
            jnp.einsum("qhd,khd->hqk", query_block, key_rows, preferred_element_type=jnp.float32)
            * 0.125
        )
        return jnp.where(key_valid[None, None, :], raw_scores, -1e30)

    def step_item(totals, packed):
        tok_rows, cot_rows, seq_length, seq_pair = packed
        scale_a = seq_pair[:model_width]
        scale_b = seq_pair[model_width:]
        key_valid = key_pos < seq_length
        inputs_f = tok_rows.astype(jnp.float32)
        norm_a = normed(inputs_f, norm_gains[0], scale_a)
        hidden_a = lax.all_gather(norm_a.astype(jnp.bfloat16), "mp", axis=0, tiled=True)
        qkv_all = jnp.einsum(
            "td,cde->cte", hidden_a, qkv_weight, preferred_element_type=jnp.float32
        ).astype(jnp.bfloat16)
        queries = qkv_all[0].reshape(seq_len, heads_dev, HEAD)
        key_rows = qkv_all[1].reshape(seq_len, heads_dev, HEAD)
        values = qkv_all[2].reshape(seq_len, heads_dev, HEAD)
        query_blocks = queries.reshape(block_count, block_rows, heads_dev, HEAD)

        def attend(query_block):
            scores = masked_scores(query_block, key_rows, key_valid)
            row_max = jnp.max(scores, axis=-1, keepdims=True)
            expo = jnp.exp(scores - row_max)
            row_sum = jnp.sum(expo, axis=-1, keepdims=True)
            probs = (expo / row_sum).astype(jnp.bfloat16)
            mixed = jnp.einsum("hqk,khd->qhd", probs, values, preferred_element_type=jnp.float32)
            return (mixed.astype(jnp.bfloat16), row_max[..., 0] + jnp.log(row_sum[..., 0]))

        mixed_blocks, log_sums = lax.map(attend, query_blocks)
        mixed_heads = mixed_blocks.reshape(seq_len, heads_dev * HEAD)
        attn_branch = lax.psum_scatter(
            jnp.dot(mixed_heads, out_weight, preferred_element_type=jnp.float32).astype(
                jnp.bfloat16
            ),
            "mp",
            scatter_dimension=0,
            tiled=True,
        ).astype(jnp.float32)
        resid = inputs_f + attn_branch
        norm_b = normed(resid, norm_gains[1], scale_b)
        hidden_b = lax.all_gather(norm_b.astype(jnp.bfloat16), "mp", axis=0, tiled=True)
        up_proj = jnp.dot(hidden_b, up_weight, preferred_element_type=jnp.float32)
        activated = exact_gelu(up_proj).astype(jnp.bfloat16)
        mlp_branch = lax.psum_scatter(
            jnp.dot(activated, down_weight, preferred_element_type=jnp.float32).astype(
                jnp.bfloat16
            ),
            "mp",
            scatter_dimension=0,
            tiled=True,
        ).astype(jnp.float32)
        layer_out = (resid + mlp_branch).astype(jnp.bfloat16)
        cot_all = lax.all_gather(cot_rows, "mp", axis=0, tiled=True)
        d_act = jnp.einsum("td,fd->tf", cot_all, down_weight, preferred_element_type=jnp.float32)
        grad_down = jnp.einsum("tf,td->fd", activated, cot_all, preferred_element_type=jnp.float32)
        gelu_out, gelu_pull = jax.vjp(exact_gelu, up_proj)
        d_up = gelu_pull(d_act)[0].astype(jnp.bfloat16)
        grad_up = jnp.einsum("td,tf->df", hidden_b, d_up, preferred_element_type=jnp.float32)
        d_norm_b = lax.psum_scatter(
            jnp.einsum("tf,df->td", d_up, up_weight, preferred_element_type=jnp.float32).astype(
                jnp.bfloat16
            ),
            "mp",
            scatter_dimension=0,
            tiled=True,
        ).astype(jnp.float32)
        norm_out_b, norm_pull_b = jax.vjp(normed, resid, norm_gains[1], scale_b)
        d_resid_ln, d_gain_b, d_scale_b = norm_pull_b(d_norm_b)
        d_resid = cot_rows.astype(jnp.float32) + d_resid_ln
        d_branch = lax.all_gather(d_resid.astype(jnp.bfloat16), "mp", axis=0, tiled=True)
        d_mixed = jnp.einsum(
            "td,ed->te", d_branch, out_weight, preferred_element_type=jnp.float32
        ).astype(jnp.bfloat16)
        grad_out = jnp.einsum(
            "te,td->ed", mixed_heads, d_branch, preferred_element_type=jnp.float32
        )
        d_mixed_blocks = d_mixed.reshape(block_count, block_rows, heads_dev, HEAD)

        def attend_back(sums, block_in):
            query_block, d_mix_block, log_block = block_in
            scores = masked_scores(query_block, key_rows, key_valid)
            probs_f = jnp.exp(scores - log_block[..., None])
            d_probs = jnp.einsum(
                "qhd,khd->hqk", d_mix_block, values, preferred_element_type=jnp.float32
            )
            inner = jnp.sum(probs_f * d_probs, axis=-1, keepdims=True)
            d_raw = (probs_f * (d_probs - inner) * 0.125).astype(jnp.bfloat16)
            d_query = jnp.einsum(
                "hqk,khd->qhd", d_raw, key_rows, preferred_element_type=jnp.float32
            )
            d_key = sums[0] + jnp.einsum(
                "hqk,qhd->khd", d_raw, query_block, preferred_element_type=jnp.float32
            )
            d_value = sums[1] + jnp.einsum(
                "hqk,qhd->khd",
                probs_f.astype(jnp.bfloat16),
                d_mix_block,
                preferred_element_type=jnp.float32,
            )
            return ((d_key, d_value), d_query)

        zero_keys = jnp.zeros((seq_len, heads_dev, HEAD), jnp.float32)
        kv_sums, d_query_blocks = lax.scan(
            attend_back, (zero_keys, zero_keys), (query_blocks, d_mixed_blocks, log_sums)
        )
        d_qkv = jnp.stack(
            [
                d_query_blocks.reshape(seq_len, heads_dev * HEAD),
                kv_sums[0].reshape(seq_len, heads_dev * HEAD),
                kv_sums[1].reshape(seq_len, heads_dev * HEAD),
            ]
        ).astype(jnp.bfloat16)
        grad_qkv = jnp.einsum("td,cte->cde", hidden_a, d_qkv, preferred_element_type=jnp.float32)
        d_norm_a = lax.psum_scatter(
            jnp.einsum("cte,cde->td", d_qkv, qkv_weight, preferred_element_type=jnp.float32).astype(
                jnp.bfloat16
            ),
            "mp",
            scatter_dimension=0,
            tiled=True,
        ).astype(jnp.float32)
        norm_out_a, norm_pull_a = jax.vjp(normed, inputs_f, norm_gains[0], scale_a)
        d_input_ln, d_gain_a, d_scale_a = norm_pull_a(d_norm_a)
        input_grad = (d_resid + d_input_ln).astype(jnp.bfloat16)
        weight_terms = (grad_qkv, grad_out, grad_up, grad_down)
        new_weights = jax.tree.map(lambda held, fresh: held + fresh, totals[0], weight_terms)
        new_gains = totals[1] + jnp.stack([d_gain_a, d_gain_b])
        d_pair = jnp.concatenate([d_scale_a, d_scale_b])
        return ((new_weights, new_gains), (layer_out, input_grad, d_pair))

    start_weights = (
        jnp.zeros(qkv_weight.shape, jnp.float32),
        jnp.zeros(out_weight.shape, jnp.float32),
        jnp.zeros(up_weight.shape, jnp.float32),
        jnp.zeros(down_weight.shape, jnp.float32),
    )
    start_gains = jnp.zeros(norm_gains.shape, jnp.float32)
    final_totals, per_item = lax.scan(
        step_item, (start_weights, start_gains), (token_items, cot_items, len_items, pairs)
    )
    weight_totals, gain_totals = final_totals
    layer_outs, input_grads, d_pairs = per_item
    weight_totals = (
        lax.psum_scatter(
            weight_totals[0].astype(jnp.bfloat16), "dp", scatter_dimension=1, tiled=True
        ).astype(jnp.float32),
        lax.psum_scatter(
            weight_totals[1].astype(jnp.bfloat16), "dp", scatter_dimension=1, tiled=True
        ).astype(jnp.float32),
        lax.psum_scatter(
            weight_totals[2].astype(jnp.bfloat16), "dp", scatter_dimension=0, tiled=True
        ).astype(jnp.float32),
        lax.psum_scatter(
            weight_totals[3].astype(jnp.bfloat16), "dp", scatter_dimension=1, tiled=True
        ).astype(jnp.float32),
    )
    time_part = jnp.dot(feats.T, d_pairs, precision=lax.Precision.HIGHEST)
    gains_grad, time_grad = (
        lax.psum_scatter(gain_totals, ("dp", "mp"), scatter_dimension=1, tiled=True),
        lax.psum_scatter(time_part, ("dp", "mp"), scatter_dimension=1, tiled=True),
    )
    return (
        layer_outs.reshape(tokens.shape),
        input_grads.reshape(tokens.shape),
        weight_totals[0],
        weight_totals[1],
        weight_totals[2],
        weight_totals[3],
        gains_grad,
        time_grad,
    )


BF = jnp.bfloat16
F32 = jnp.float32
VMEM_LIMIT = 62 << 20
EXP_SCALE = 0.125 * math.log2(math.e)
HOLD = pl.Buffered(1)
ANY = pl.BlockSpec(memory_space=pl.ANY)


def contract(left, right, left_dim, right_dim):
    return lax.dot_general(
        left, right, (((left_dim,), (right_dim,)), ((), ())), preferred_element_type=F32
    )


def call(
    body, meta, args, grid, in_specs, out_specs, out_shape, flops, scratch=(), aliases=None, weight=0.5
):
    moved = sum(a.size * a.dtype.itemsize for a in args)
    moved += sum(math.prod(o.shape) * jnp.dtype(o.dtype).itemsize for o in out_shape)
    return pl.pallas_call(
        body,
        grid_spec=pltpu.PrefetchScalarGridSpec(
            num_scalar_prefetch=1,
            grid=grid,
            in_specs=in_specs,
            out_specs=out_specs,
            scratch_shapes=list(scratch),
        ),
        out_shape=out_shape,
        input_output_aliases=aliases or {},
        compiler_params=pltpu.CompilerParams(vmem_limit_bytes=VMEM_LIMIT),
        cost_estimate=pl.CostEstimate(
            flops=int(flops * weight), bytes_accessed=int(moved * 0.01), transcendentals=0
        ),
    )(meta, *args)


def shape(dims, kind=BF):
    return jax.ShapeDtypeStruct(tuple(dims), kind)


def normalize(values):
    center = values - jnp.mean(values, axis=-1, keepdims=True)
    spread = jnp.mean(center * center, axis=-1, keepdims=True)
    root = lax.rsqrt(spread + 1e-05)
    return center * root, root


def norm_back(d_out, unit, root, gain):
    d_unit = d_out * gain
    return root * (
        d_unit
        - jnp.mean(d_unit, axis=-1, keepdims=True)
        - unit * jnp.mean(d_unit * unit, axis=-1, keepdims=True)
    )


def first_proj(meta, s, tok, recv, gain, weight, prev):
    _, rows, width = tok.shape
    part = weight.shape[2]
    seqs = gain.shape[0]

    def body(m, loc, rec, g, w, *refs):
        tokf, hid, qkv = refs[-3:]

        @pl.when(pl.program_id(0) == m[0])
        def _():
            tokf[0] = loc[0]

        @pl.when(pl.program_id(0) != m[0])
        def _():
            tokf[0] = rec[0]

        unit, _ = normalize(tokf[0].astype(F32))
        hidden = (unit * g[0]).astype(BF)
        hid[0] = hidden
        for c in range(3):
            qkv[0, c] = contract(w[c], hidden, 0, 1).astype(BF)

    length = 2 * rows
    outs = [shape((seqs, length, width)), shape((seqs, length, width)), shape((seqs, 3, part, length))]
    return call(
        body,
        meta,
        [tok, recv, gain, weight] + list(prev),
        (2,),
        [
            pl.BlockSpec((1, rows, width), lambda h, m: (m[1 + s], 0, 0)),
            pl.BlockSpec((1, rows, width), lambda h, m: (0, 0, 0)),
            pl.BlockSpec((1, 1, width), lambda h, m: (s, 0, 0)),
            pl.BlockSpec((3, width, part), lambda h, m: (0, 0, 0), pipeline_mode=HOLD),
        ]
        + [ANY] * len(prev),
        [
            pl.BlockSpec((1, rows, width), lambda h, m: (s, h, 0)),
            pl.BlockSpec((1, rows, width), lambda h, m: (s, h, 0)),
            pl.BlockSpec((1, 3, part, rows), lambda h, m: (s, 0, 0, h)),
        ],
        outs,
        6 * length * width * part,
        weight=0.8,
        aliases={5 + i: i for i in range(len(prev))},
    )


def other_proj(meta, hid, weight, s, prev):
    seqs, length, width = hid.shape
    part = weight.shape[2]
    rows = length // 2

    def body(m, h_ref, w, *refs):
        for c in range(3):
            refs[-1][0, c] = contract(w[c], h_ref[0], 0, 1).astype(BF)

    return call(
        body,
        meta,
        [hid, weight] + list(prev),
        (2,),
        [
            pl.BlockSpec((1, rows, width), lambda h, m: (s, h, 0)),
            pl.BlockSpec((3, width, part), lambda h, m: (0, 0, 0), pipeline_mode=HOLD),
        ]
        + [ANY] * len(prev),
        [pl.BlockSpec((1, 3, part, rows), lambda h, m: (s, 0, 0, h))],
        [shape((seqs, 3, part, length))],
        6 * length * width * part,
        weight=0.8,
        aliases={3 + i: i for i in range(len(prev))},
    )


def mask_rows(valid, extent, block):
    first = lax.broadcasted_iota(jnp.int32, (16, extent), 0) == 0
    hidden = lax.broadcasted_iota(jnp.int32, (16, extent), 1) >= valid
    keys = jnp.where(first & hidden, -1e30, 0.0).astype(BF)
    ones = jnp.where(lax.broadcasted_iota(jnp.int32, (16, block), 0) == 0, 1.0, 0.0).astype(BF)
    return keys, ones


def by_extent(valid, length, work):
    step = min(256, length)
    for extent in range(step, length + 1, step):
        low = extent - step if extent > step else -1
        high = extent if extent < length else length * 2

        @pl.when((valid > low) & (valid <= high))
        def _():
            work(extent)


def attention(meta, qkv, first, count, prev):
    seqs, _, part, length = qkv.shape
    heads = part // HEAD
    view = qkv.reshape(seqs, 3, heads, HEAD, length)
    lens_at = 1 + seqs

    def body(m, q, k, v, *refs):
        out, logs = refs[-2:]
        valid = m[lens_at + first + pl.program_id(0)]

        def work(extent):
            key_mask, ones = mask_rows(valid, extent, length)
            keys = jnp.concatenate([k[0, 0, 0, :, :extent], key_mask], 0)
            scores = contract(keys, jnp.concatenate([q[0, 0, 0], ones], 0), 0, 0)
            top = jnp.max(scores, 0, keepdims=True)
            expo = jnp.exp2((scores - top) * EXP_SCALE)
            total = jnp.sum(expo, 0, keepdims=True)
            mixed = contract(v[0, 0, 0, :, :extent], expo.astype(BF), 1, 0)
            out[0, 0] = (mixed / total).astype(BF)
            logs[0, 0] = top * EXP_SCALE + jnp.log2(total)

        by_extent(valid, length, work)

    def spec(c):
        return pl.BlockSpec((1, 1, 1, HEAD, length), lambda s, h, m: (s + first, c, h, 0, 0))

    return call(
        body,
        meta,
        [view, view, view] + list(prev),
        (count, heads),
        [spec(0), spec(1), spec(2)] + [ANY] * len(prev),
        [
            pl.BlockSpec((1, 1, HEAD, length), lambda s, h, m: (s + first, h, 0, 0)),
            pl.BlockSpec((1, 1, 1, length), lambda s, h, m: (s + first, h, 0, 0)),
        ],
        [shape((seqs, heads, HEAD, length)), shape((seqs, heads, 1, length), F32)],
        16 * count * heads * length * length * HEAD,
        aliases={4 + i: i for i in range(len(prev))},
    )


def attention_back(meta, qkv, out, d_out, logs, first, prev):
    seqs, _, part, length = qkv.shape
    heads = part // HEAD
    view = qkv.reshape(seqs, 3, heads, HEAD, length)
    lens_at = 1 + seqs
    block = min(256, length)
    group = 2 if heads % 2 == 0 else 1

    def body(m, q, k, v, o, do, ls, *refs):
        d_qkv, dk_sum, dv_sum = refs[-3:]
        valid = m[lens_at + first]

        def work(extent):
            key_mask, ones = mask_rows(valid, extent, block)
            for h in range(group):
                keys = k[0, 0, h, :, :extent]
                vals = v[0, 0, h, :, :extent]
                masked_keys = jnp.concatenate([keys, key_mask], 0)
                for i in range(length // block):
                    sl = slice(i * block, (i + 1) * block)
                    query = q[0, 0, h, :, sl]
                    d_mix = do[0, h, :, sl]
                    scores = contract(masked_keys, jnp.concatenate([query, ones], 0), 0, 0)
                    probs = jnp.exp2(scores * EXP_SCALE - ls[0, h, :, sl])
                    inner = jnp.sum(d_mix.astype(F32) * o[0, h, :, sl].astype(F32), 0, keepdims=True)
                    d_probs = contract(vals, d_mix, 0, 0)
                    d_raw = (probs * (d_probs - inner) * 0.125).astype(BF)
                    d_value = contract(d_mix, probs.astype(BF), 1, 1)
                    d_key = contract(query, d_raw, 1, 1)
                    if i == 0:
                        dk_sum[:, :extent] = d_key
                        dv_sum[:, :extent] = d_value
                    else:
                        dk_sum[:, :extent] += d_key
                        dv_sum[:, :extent] += d_value
                    d_qkv[0, 0, h, :, sl] = contract(keys, d_raw, 1, 0).astype(BF)
                d_qkv[0, 1, h, :, :extent] = dk_sum[:, :extent].astype(BF)
                d_qkv[0, 2, h, :, :extent] = dv_sum[:, :extent].astype(BF)
                if extent < length:
                    rest = jnp.zeros((HEAD, length - extent), BF)
                    d_qkv[0, 1, h, :, extent:] = rest
                    d_qkv[0, 2, h, :, extent:] = rest

        by_extent(valid, length, work)

    def spec(c):
        return pl.BlockSpec((1, 1, group, HEAD, length), lambda h, m: (first, c, h, 0, 0))

    head_spec = pl.BlockSpec((1, group, HEAD, length), lambda h, m: (first, h, 0, 0))
    return call(
        body,
        meta,
        [view, view, view, out, d_out, logs] + list(prev),
        (heads // group,),
        [
            spec(0),
            spec(1),
            spec(2),
            head_spec,
            head_spec,
            pl.BlockSpec((1, group, 1, length), lambda h, m: (first, h, 0, 0)),
        ]
        + [ANY] * len(prev),
        [pl.BlockSpec((1, 3, group, HEAD, length), lambda h, m: (first, 0, h, 0, 0))],
        [shape((seqs, 3, heads, HEAD, length))],
        40 * heads * length * length * HEAD,
        weight=0.02,
        scratch=[pltpu.VMEM((HEAD, length), F32)] * 2,
        aliases={7 + i: i for i in range(len(prev))},
    )


def out_proj(meta, own_mix, oth_mix, tokf, own_w, oth_w, gain):
    seqs, length, width = tokf.shape
    rows = length // 2
    part = own_w.shape[0]
    own_mix = own_mix.reshape(seqs, part, length)
    oth_mix = oth_mix.reshape(seqs, part, length)

    def body(m, a, b, t, wa, wb, g, resid, hid):
        branch = contract(a[0], wa[...], 0, 0) + contract(b[0], wb[...], 0, 0)
        total = t[0].astype(F32) + branch
        resid[0] = total.astype(BF)
        unit, _ = normalize(total)
        hid[0] = (unit * g[0]).astype(BF)

    mix_spec = pl.BlockSpec((1, part, rows), lambda s, h, m: (s, 0, h))
    row_spec = pl.BlockSpec((1, rows, width), lambda s, h, m: (s, h, 0))
    w_spec = pl.BlockSpec((part, width), lambda s, h, m: (0, 0), pipeline_mode=HOLD)
    return call(
        body,
        meta,
        [own_mix, oth_mix, tokf, own_w, oth_w, gain],
        (seqs, 2),
        [
            mix_spec,
            mix_spec,
            row_spec,
            w_spec,
            w_spec,
            pl.BlockSpec((1, 1, width), lambda s, h, m: (s, 0, 0)),
        ],
        [row_spec] * 2,
        [shape((seqs, length, width))] * 2,
        4 * seqs * length * width * part,
    )


def feed_forward(meta, hid, cot, cot_recv, up_w, down_w):
    seqs, length, width = hid.shape
    tokens = seqs * length
    hidden = up_w.shape[1]
    block = min(512, hidden)
    rows = min(1024, tokens)
    steps = hidden // block
    half_root = 1.0 / math.sqrt(2.0)
    density = 1.0 / math.sqrt(2.0 * math.pi)

    def body(m, h_ref, stay, came, wu, wd, out, d_hid, grads, act, d_up, out_sum, hid_sum, c_ref, stage, sem):
        step = pl.program_id(0)

        def loads():
            moves = []
            for s in range(seqs):
                for k, src in enumerate((stay.at[m[1 + s]], came.at[s])):
                    half = m[0] if k == 0 else 1 - m[0]
                    at = pl.multiple_of(s * length + half * (length // 2), length // 2)
                    dst = c_ref.at[pl.ds(at, length // 2)]
                    moves.append(pltpu.make_async_copy(src, dst, sem.at[s, k]))
            return moves

        def stores():
            return [
                pltpu.make_async_copy(stage.at[0], out, sem.at[seqs, 0]),
                pltpu.make_async_copy(stage.at[1], d_hid, sem.at[seqs, 1]),
            ]

        @pl.when(step == 0)
        def _():
            for move in loads():
                move.start()
            out_sum[...] = jnp.zeros_like(out_sum)
            hid_sum[...] = jnp.zeros_like(hid_sum)
            for move in loads():
                move.wait()

        for r in range(tokens // rows):
            sl = slice(r * rows, (r + 1) * rows)
            up = contract(h_ref[sl, :], wu[...], 1, 0)
            d_act = contract(c_ref[sl, :], wd[...], 1, 1)
            cdf = 0.5 * (1.0 + lax.erf(up * half_root))
            slope = cdf + up * (density * jnp.exp(-0.5 * up * up))
            a = (up * cdf).astype(BF)
            d = (d_act * slope).astype(BF)
            act[sl, :] = a
            d_up[sl, :] = d
            out_sum[sl, :] += contract(a, wd[...], 1, 0)
            hid_sum[sl, :] += contract(d, wu[...], 1, 1)

        @pl.when(step == steps - 1)
        def _():
            stage[0] = out_sum[...].astype(BF)
            stage[1] = hid_sum[...].astype(BF)
            for move in stores():
                move.start()

        grads[0] = contract(h_ref[...], d_up[...], 0, 0).astype(BF)
        grads[1] = contract(c_ref[...], act[...], 0, 0).astype(BF)

        @pl.when(step == steps - 1)
        def _():
            for move in stores():
                move.wait()

    return call(
        body,
        meta,
        [hid.reshape(tokens, width), cot, cot_recv, up_w, down_w],
        (steps,),
        [
            pl.BlockSpec((tokens, width), lambda j, m: (0, 0), pipeline_mode=HOLD),
            ANY,
            ANY,
            pl.BlockSpec((width, block), lambda j, m: (0, j)),
            pl.BlockSpec((block, width), lambda j, m: (j, 0)),
        ],
        [ANY, ANY, pl.BlockSpec((2, width, block), lambda j, m: (0, 0, j))],
        [shape((tokens, width)), shape((tokens, width)), shape((2, width, hidden))],
        12 * tokens * width * hidden,
        weight=0.4,
        scratch=[
            pltpu.VMEM((tokens, block), BF),
            pltpu.VMEM((tokens, block), BF),
            pltpu.VMEM((tokens, width), F32),
            pltpu.VMEM((tokens, width), F32),
            pltpu.VMEM((tokens, width), BF),
            pltpu.VMEM((2, tokens, width), BF),
            pltpu.SemaphoreType.DMA((seqs + 1, 2)),
        ],
    )


def middle(meta, resid, mlp, d_hid, cot, cot_recv, own_mix, oth_mix, own_w, oth_w, gain):
    items = cot.shape[0]
    seqs, length, width = resid.shape
    rows = length // 2
    part = own_w.shape[0]
    mixes = [a.reshape(seqs, part, length) for a in (own_mix, oth_mix)]
    parts = [a.reshape(resid.shape) for a in mlp + d_hid]

    def body(
        m, res, up, up2, dh, dh2, cl, cr, ma, mb, wa, wb, g, mine, away, branch, dma, dmb, grad, gsum, grad_sum, vec, ct
    ):
        phase, s = pl.program_id(0), pl.program_id(1)

        @pl.when((phase == 0) & (s == 0))
        def _():
            grad_sum[...] = jnp.zeros_like(grad_sum)
            vec[...] = jnp.zeros_like(vec)

        resid_f = res[0].astype(F32)
        total = (resid_f + (up[0].astype(F32) + up2[0].astype(F32))).astype(BF)

        @pl.when(phase == 0)
        def _():
            away[0] = total
            ct[...] = cr[0]

        @pl.when(phase == 1)
        def _():
            mine[0] = total
            ct[...] = cl[0]

        unit, root = normalize(resid_f)
        d_out = dh[0].astype(F32) + dh2[0].astype(F32)
        vec[s] += jnp.sum(d_out * unit, axis=0, keepdims=True)
        d_res = (ct[...].astype(F32) + norm_back(d_out, unit, root, g[0])).astype(BF)
        branch[0] = d_res
        dma[0] = contract(wa[...], d_res, 1, 1).astype(BF)
        dmb[0] = contract(wb[...], d_res, 1, 1).astype(BF)
        grad_sum[0] += contract(d_res, ma[0], 0, 1)
        grad_sum[1] += contract(d_res, mb[0], 0, 1)

        @pl.when((phase == 1) & (s == seqs - 1))
        def _():
            grad[...] = grad_sum[...].astype(BF)
            gsum[...] = vec[...]

    def at(p, m):
        return (1 - m[0]) + p * (2 * m[0] - 1)

    row_spec = pl.BlockSpec((1, rows, width), lambda p, s, m: (s, at(p, m), 0))
    mix_spec = pl.BlockSpec((1, part, rows), lambda p, s, m: (s, 0, at(p, m)))
    w_spec = pl.BlockSpec((part, width), lambda p, s, m: (0, 0), pipeline_mode=HOLD)
    return call(
        body,
        meta,
        [resid] + parts + [cot, cot_recv, mixes[0], mixes[1], own_w, oth_w, gain],
        (2, seqs),
        [row_spec] * 5
        + [
            pl.BlockSpec((1, rows, width), lambda p, s, m: (m[1 + p * s], 0, 0)),
            pl.BlockSpec((1, rows, width), lambda p, s, m: (s + p * (seqs - 1 - s), 0, 0)),
        ]
        + [mix_spec] * 2
        + [w_spec] * 2
        + [pl.BlockSpec((1, 1, width), lambda p, s, m: (s, 0, 0))],
        [
            pl.BlockSpec((1, rows, width), lambda p, s, m: (m[1 + p * s], 0, 0)),
            pl.BlockSpec((1, rows, width), lambda p, s, m: (s + p * (seqs - 1 - s), 0, 0)),
            row_spec,
            mix_spec,
            mix_spec,
            pl.BlockSpec((2, width, part), lambda p, s, m: (0, 0, 0), pipeline_mode=HOLD),
            pl.BlockSpec((seqs, 1, width), lambda p, s, m: (0, 0, 0)),
        ],
        [
            shape((items, rows, width)),
            shape((seqs, rows, width)),
            shape((seqs, length, width)),
            shape((seqs, part, length)),
            shape((seqs, part, length)),
            shape((2, width, part)),
            shape((seqs, 1, width), F32),
        ],
        8 * seqs * length * width * part,
        weight=1.0,
        scratch=[
            pltpu.VMEM((2, width, part), F32),
            pltpu.VMEM((seqs, 1, width), F32),
            pltpu.VMEM((rows, width), BF),
        ],
    )


def proj_grad(meta, hid, d_qkv):
    seqs, length, width = hid.shape
    part = d_qkv.shape[2] * d_qkv.shape[3]
    d_qkv = d_qkv.reshape(seqs, 3, part, length)

    def body(m, h_ref, d_ref, grad):
        total = contract(d_ref[0, 0], h_ref[0], 1, 0)
        for s in range(1, seqs):
            total += contract(d_ref[s, 0], h_ref[s], 1, 0)
        grad[0] = total.astype(BF).T

    return call(
        body,
        meta,
        [hid, d_qkv],
        (3,),
        [
            pl.BlockSpec((seqs, length, width), lambda c, m: (0, 0, 0), pipeline_mode=HOLD),
            pl.BlockSpec((seqs, 1, part, length), lambda c, m: (0, c, 0, 0)),
        ],
        [pl.BlockSpec((1, width, part), lambda c, m: (c, 0, 0))],
        [shape((3, width, part))],
        6 * seqs * length * width * part,
        weight=0.02,
    )[0]


def input_back(meta, tokf, branch, own_d, oth_d, own_w, oth_w, gain, items, stay, s, prev):
    seqs, length, width = tokf.shape
    rows = length // 2
    part = own_w.shape[2]
    block = min(256, rows)
    cuts = rows // block
    own_d = own_d.reshape(seqs, 3, part, length)
    oth_d = oth_d.reshape(seqs, 3, part, length)

    def body(m, tok, br, da, db, wa, wb, g, *refs):
        out, gsum = refs[-2:]
        d_hid = contract(da[0, 0], wa[0], 0, 1) + contract(db[0, 0], wb[0], 0, 1)
        for c in range(1, 3):
            d_hid += contract(da[0, c], wa[c], 0, 1) + contract(db[0, c], wb[c], 0, 1)
        unit, root = normalize(tok[0].astype(F32))
        vec = jnp.sum(d_hid * unit, axis=0, keepdims=True)

        @pl.when(pl.program_id(0) == 0)
        def _():
            gsum[0] = vec

        @pl.when(pl.program_id(0) > 0)
        def _():
            gsum[0] += vec

        out[0] = (br[0].astype(F32) + norm_back(d_hid, unit, root, g[0])).astype(BF)

    def at(i, m):
        return (m[0] if stay else 1 - m[0]) * cuts + i

    row_spec = pl.BlockSpec((1, block, width), lambda i, m: (s, at(i, m), 0))
    d_spec = pl.BlockSpec((1, 3, part, block), lambda i, m: (s, 0, 0, at(i, m)))
    w_spec = pl.BlockSpec((3, width, part), lambda i, m: (0, 0, 0), pipeline_mode=HOLD)
    return call(
        body,
        meta,
        [tokf, branch, own_d, oth_d, own_w, oth_w, gain] + list(prev),
        (cuts,),
        [row_spec, row_spec, d_spec, d_spec, w_spec, w_spec]
        + [pl.BlockSpec((1, 1, width), lambda i, m: (s, 0, 0))]
        + [ANY] * len(prev),
        [
            pl.BlockSpec((1, block, width), lambda i, m: (m[1 + s] if stay else 0, i, 0)),
            pl.BlockSpec((1, 1, width), lambda i, m: (0, 0, 0)),
        ],
        [shape((items if stay else 1, rows, width)), shape((1, 1, width), F32)],
        12 * rows * width * part,
        weight=0.02,
        aliases={8 + i: i for i in range(len(prev))},
    )


def place(meta, base, came, first, seqs):
    count, rows, width = came.shape
    at = 1 + 2 * seqs + first

    def body(m, src, _, out):
        out[...] = src[...]

    return call(
        body,
        meta,
        [came, base],
        (count,),
        [pl.BlockSpec((1, rows, width), lambda s, m: (s, 0, 0)), ANY],
        [pl.BlockSpec((1, rows, width), lambda s, m: (m[at + s], 0, 0))],
        [shape(base.shape)],
        1,
        aliases={2: 0},
    )[0]


def after(value, *earlier):
    return lax.optimization_barrier((value,) + earlier)[0]


def per_device_pair(
    tokens,
    lengths,
    timesteps,
    norm_gains,
    time_weight,
    qkv_weight,
    out_weight,
    up_weight,
    down_weight,
    cotangent,
):
    micro_count, seq_dev, rows, width = tokens.shape
    items = micro_count * seq_dev
    seqs = items // 2
    x = lax.axis_index("mp")
    dp = lax.axis_index("dp")
    dp_count = lax.axis_size("dp")
    part = qkv_weight.shape[2]
    hidden = up_weight.shape[1]
    tok = tokens.reshape(items, rows, width)
    cot = cotangent.reshape(items, rows, width)
    lens = lengths.reshape(items)
    steps = timesteps.reshape(items)

    at = jnp.arange(items, dtype=jnp.int32)
    longer = (lens[None, :] > lens[:, None]) | (
        (lens[None, :] == lens[:, None]) & (at[None, :] < at[:, None])
    )
    rank = jnp.sum(longer.astype(jnp.int32), axis=1)
    holder = (rank + 1) // 2 % 2
    slot = rank // 2

    def chosen(device, values):
        hit = (holder == device)[None, :] & (slot[None, :] == jnp.arange(seqs)[:, None])
        return jnp.sum(jnp.where(hit, values[None, :], 0), axis=1)

    own, oth = chosen(x, at), chosen(1 - x, at)
    meta = jnp.concatenate([x[None], own, chosen(x, lens), oth]).astype(jnp.int32)

    def swap(value):
        return lax.ppermute(value, "mp", [(0, 1), (1, 0)])

    def shard(value):
        count = value.shape[0] // dp_count
        return lax.dynamic_slice_in_dim(value, dp * count, count, 0)

    def spread(value):
        return lax.all_gather(value, "dp", axis=0, tiled=True)

    qkv_rows = qkv_weight.reshape(3 * width, part)
    def sent(rows_of, s):
        return lax.dynamic_slice_in_dim(rows_of, oth[s], 1, 0)

    tok_first = sent(tok, 0)
    tok_recv = [swap(tok_first)]
    qkv_shard = swap(after(shard(qkv_rows), tok_first))
    qkv_oth = spread(qkv_shard).reshape(qkv_weight.shape)

    feats = sinusoid(chosen(x, steps))
    pairs = jnp.dot(feats, time_weight, precision=lax.Precision.HIGHEST)
    widened = 1.0 + pairs.reshape(seqs, 2, 1, width)
    gain_a = norm_gains[0] * widened[:, 0]
    gain_b = norm_gains[1] * widened[:, 1]

    near = [shard(w).reshape(-1, width) for w in (out_weight, up_weight, down_weight)]
    far = swap(after(jnp.concatenate(near, 0), tok_recv[0]))
    base, qkv_far, mix_own, mix_oth = (), (), (), ()
    for s in range(seqs):
        head = s == 0
        base = first_proj(meta, s, tok, tok_recv[s], gain_a, qkv_weight, base)
        mix_own = attention(meta, base[2], s, 1, mix_own)
        if s + 1 < seqs:
            tok_recv.append(swap(after(sent(tok, s + 1), tok_recv[s])))
        order = after(meta, far) if head else meta
        qkv_far = other_proj(order, base[1], qkv_oth, s, qkv_far)
        if head:
            arrived = after(far, base[2])
            cuts = [0]
            for piece in near:
                cuts.append(cuts[-1] + piece.shape[0])
            out_oth, up_oth, down_oth = [
                spread(arrived[cuts[i] : cuts[i + 1]].reshape(w.shape[0] // dp_count, w.shape[1]))
                for i, w in enumerate((out_weight, up_weight, down_weight))
            ]
        mix_oth = attention(meta, qkv_far[0], s, 1, mix_oth)
        if head:
            cot_sent = jnp.concatenate([sent(cot, i) for i in range(seqs)], 0)
            cot_recv = swap(after(cot_sent, tok_recv[-1]))
    tokf, hid_a, qkv_own = base
    qkv_far = qkv_far[0]
    resid, hid_b = out_proj(meta, mix_own[0], mix_oth[0], tokf, out_weight, out_oth, gain_b)
    mlp_own, back_own, grads_own = feed_forward(meta, hid_b, cot, cot_recv, up_weight, down_weight)
    mlp_oth, back_oth, grads_oth = feed_forward(
        after(meta, grads_own), hid_b, cot, cot_recv, up_oth, down_oth
    )

    def tree_send(value, step):
        count, cols = value.shape[0], value.shape[-1]
        value = value.reshape(count, -1, 1, 2, width // dp_count, cols)
        mine_at = dp // step % 2
        keep = lax.dynamic_index_in_dim(value, mine_at, 3, False)
        send = lax.dynamic_index_in_dim(value, 1 - mine_at, 3, False)
        return keep, lax.ppermute(send, "dp", [(i, i ^ step) for i in range(dp_count)])

    def tree_add(pair, gate):
        keep, came = pair[0], after(pair[1], *gate)
        return (keep.astype(F32) + came.astype(F32)).astype(BF)

    def tree(value):
        step = 1
        while step * 4 < dp_count:
            pair = tree_send(value, step)
            value = tree_add(pair, (yield value))
            step *= 2
        left = dp_count // step
        held = value
        value = value.reshape(value.shape[0], left, width // dp_count, value.shape[-1])
        place_at = dp // step

        def piece(k):
            return lax.dynamic_index_in_dim(value, place_at ^ k, 1, False)

        came = [
            lax.ppermute(piece(k), "dp", [(i, i ^ (k * step)) for i in range(dp_count)])
            for k in range(1, left)
        ]
        gate = yield held
        total = piece(0).astype(F32)
        for part_in in came:
            total += after(part_in, *gate).astype(F32)
        yield total.astype(BF)

    def reduce(value):
        return lax.psum_scatter(value, "dp", scatter_dimension=1, tiled=True)

    ffn_own = reduce(grads_own)
    ffn_oth = reduce(grads_oth)
    out_stay, out_away, branch, d_mix_own, d_mix_oth, out_grads, sum_b = middle(
        meta,
        resid,
        [mlp_own, mlp_oth],
        [back_own, back_oth],
        cot,
        cot_recv,
        mix_own[0],
        mix_oth[0],
        out_weight,
        out_oth,
        gain_b,
    )
    out_came = []

    def heads_view(value):
        return value.reshape(seqs, part // HEAD, HEAD, 2 * rows)

    class Job:
        def __init__(self, value):
            self.run, self.value, self.done = tree(value), None, False
            self.value = next(self.run)

        def go(self, *gate):
            if not self.done:
                try:
                    self.value = self.run.send(gate)
                except StopIteration:
                    self.done = True
            return self.value

    d_mix_own, d_mix_oth = heads_view(d_mix_own), heads_view(d_mix_oth)
    out_job = Job(out_grads)
    d_oth, d_own = (), ()
    order = meta
    for s in range(seqs):
        d_oth = attention_back(order, qkv_far, mix_oth[0], d_mix_oth, mix_oth[1], s, d_oth)
        order = after(meta, out_job.go(d_oth[0]))
    grad_oth = proj_grad(order, hid_a, d_oth[0])
    oth_job = Job(grad_oth)
    order = after(meta, grad_oth, ffn_own)
    for s in range(seqs):
        out_came.append(swap(after(out_away[s : s + 1], d_own[0] if s else grad_oth)))
        d_own = attention_back(order, qkv_own, mix_own[0], d_mix_own, mix_own[1], s, d_own)
        order = after(meta, oth_job.go(d_own[0]), out_came[s])
        if s == seqs - 1:
            order = after(order, out_job.go(d_own[0]))
    grad_own = proj_grad(order, hid_a, d_own[0])
    own_job = Job(grad_own)
    order = after(meta, grad_own, ffn_oth)
    in_away, in_stay, sum_a = [], (), []

    def last_back(order, s, stay, prev):
        return input_back(
            order, tokf, branch, d_own[0], d_oth[0], qkv_weight, qkv_oth, gain_a, items, stay, s, prev
        )

    for s in range(seqs):
        rows_out, vec = last_back(order, s, False, ())
        in_away.append(swap(rows_out))
        sum_a.append(vec)
        order = after(meta, rows_out, own_job.go(rows_out) if s == 0 else oth_job.go(rows_out))
    out_red, qkv_red_oth = out_job.value, oth_job.value
    far_grads = swap(
        jnp.concatenate([ffn_oth[0], ffn_oth[1], out_red[1]] + [qkv_red_oth[c] for c in range(3)], 1)
    )
    for s in range(seqs):
        rows_out, vec = last_back(order, s, True, in_stay)
        in_stay = (rows_out,)
        sum_a[s] += vec
        order = after(meta, own_job.go(rows_out) if s == 0 else rows_out)
    sum_a = jnp.concatenate(sum_a, 0)
    output, input_grad = out_stay, in_stay[0]
    for s in range(seqs):
        output = place(order, output, out_came[s], s, seqs)
        input_grad = place(order, input_grad, in_away[s], s, seqs)

    sums = jnp.stack([sum_a, sum_b], 0)[:, :, 0]
    d_pair = sums * norm_gains[:, None, :]
    gain_part = jnp.sum(sums * jnp.swapaxes(widened[:, :, 0], 0, 1), axis=1)
    count = 2 * dp_count
    cols, gain_cols, time_cols = 2 * width // count, width // count, feats.shape[1]
    by_pair = jnp.moveaxis(d_pair.reshape(2, seqs, dp_count, cols), 1, 2).reshape(count, seqs * cols)
    by_gain = jnp.moveaxis(gain_part.reshape(2, count, gain_cols), 0, 1).reshape(count, 2 * gain_cols)
    by_feat = jnp.broadcast_to(feats.reshape(1, seqs * time_cols), (count, seqs * time_cols))
    packed = jnp.concatenate([by_pair, by_gain, by_feat], 1)
    packed = after(packed, *in_away)
    everyone = lax.all_to_all(packed, ("dp", "mp"), 0, 0, tiled=True)
    far_grads = after(far_grads, everyone)
    while not own_job.done:
        own_job.go(everyone)
    everyone = after(everyone, output, input_grad)
    mine = everyone[:, : seqs * cols].reshape(count * seqs, cols)
    gains_grad = jnp.sum(everyone[:, seqs * cols :][:, : 2 * gain_cols], axis=0).reshape(2, gain_cols)
    all_feats = everyone[:, seqs * cols + 2 * gain_cols :].reshape(count * seqs, time_cols)
    time_grad = jnp.dot(all_feats.T, mine, precision=lax.Precision.HIGHEST)
    def joined(near, first, cols):
        return near.astype(F32) + far_grads[:, first : first + cols].astype(F32)

    up_sum = joined(ffn_own[0], 0, hidden)
    down_sum = joined(ffn_own[1], hidden, hidden)
    out_sum = joined(out_red[0], 2 * hidden, part)
    qkv_sum = jnp.stack(
        [joined(own_job.value[c], 2 * hidden + (1 + c) * part, part) for c in range(3)], 0
    )

    return (
        output.reshape(tokens.shape),
        input_grad.reshape(tokens.shape),
        qkv_sum,
        out_sum.T,
        up_sum,
        down_sum.T,
        gains_grad,
        time_grad,
    )


def solution(mesh):
    in_specs = (
        P(None, "dp", "mp", None),
        P(None, "dp"),
        P(None, "dp"),
        P(),
        P(),
        P(None, None, "mp"),
        P("mp", None),
        P(None, "mp"),
        P("mp", None),
        P(None, "dp", "mp", None),
    )
    out_specs = (
        P(None, "dp", "mp", None),
        P(None, "dp", "mp", None),
        P(None, "dp", "mp"),
        P("mp", "dp"),
        P("dp", "mp"),
        P("mp", "dp"),
        P(None, ("dp", "mp")),
        P(None, ("dp", "mp")),
    )
    dp_count = mesh.shape["dp"]
    paired = mesh.shape["mp"] == 2 and dp_count & (dp_count - 1) == 0
    return jax.shard_map(
        per_device_pair if paired else per_device, mesh=mesh, in_specs=in_specs, out_specs=out_specs, check_vma=False
    )
```

```python
import math

import jax
import jax.numpy as jnp
from jax import lax
from jax.experimental import pallas as pl
from jax.experimental.pallas import tpu as pltpu
from jax.sharding import PartitionSpec as P

HEAD = 64
TEMB = 256


def sinusoid(step_ids):
    half_width = TEMB // 2
    freqs = jnp.exp(-math.log(10000.0) * jnp.arange(half_width, dtype=jnp.float32) / half_width)
    angles = step_ids.astype(jnp.float32)[:, None] * freqs[None, :]
    return jnp.concatenate([jnp.sin(angles), jnp.cos(angles)], axis=1)


def normed(values, gain, scale):
    center = values - jnp.mean(values, axis=-1, keepdims=True)
    spread = jnp.mean(center * center, axis=-1, keepdims=True)
    return center * lax.rsqrt(spread + 1e-05) * gain * (1.0 + scale)


def exact_gelu(values):
    return jax.nn.gelu(values, approximate=False)


def per_device(
    tokens,
    lengths,
    timesteps,
    norm_gains,
    time_weight,
    qkv_weight,
    out_weight,
    up_weight,
    down_weight,
    cotangent,
):
    micro_count, seq_dev, row_count, model_width = tokens.shape
    item_count = micro_count * seq_dev
    seq_len = row_count * lax.axis_size("mp")
    heads_dev = qkv_weight.shape[2] // HEAD
    block_rows = min(512, seq_len)
    block_count = seq_len // block_rows
    key_pos = jnp.arange(seq_len)
    feats = sinusoid(timesteps.reshape(item_count))
    pairs = jnp.dot(feats, time_weight, precision=lax.Precision.HIGHEST)
    token_items = tokens.reshape(item_count, row_count, model_width)
    cot_items = cotangent.reshape(item_count, row_count, model_width)
    len_items = lengths.reshape(item_count)

    def masked_scores(query_block, key_rows, key_valid):
        raw_scores = (
            jnp.einsum("qhd,khd->hqk", query_block, key_rows, preferred_element_type=jnp.float32)
            * 0.125
        )
        return jnp.where(key_valid[None, None, :], raw_scores, -1e30)

    def step_item(totals, packed):
        tok_rows, cot_rows, seq_length, seq_pair = packed
        scale_a = seq_pair[:model_width]
        scale_b = seq_pair[model_width:]
        key_valid = key_pos < seq_length
        inputs_f = tok_rows.astype(jnp.float32)
        norm_a = normed(inputs_f, norm_gains[0], scale_a)
        hidden_a = lax.all_gather(norm_a.astype(jnp.bfloat16), "mp", axis=0, tiled=True)
        qkv_all = jnp.einsum(
            "td,cde->cte", hidden_a, qkv_weight, preferred_element_type=jnp.float32
        ).astype(jnp.bfloat16)
        queries = qkv_all[0].reshape(seq_len, heads_dev, HEAD)
        key_rows = qkv_all[1].reshape(seq_len, heads_dev, HEAD)
        values = qkv_all[2].reshape(seq_len, heads_dev, HEAD)
        query_blocks = queries.reshape(block_count, block_rows, heads_dev, HEAD)

        def attend(query_block):
            scores = masked_scores(query_block, key_rows, key_valid)
            row_max = jnp.max(scores, axis=-1, keepdims=True)
            expo = jnp.exp(scores - row_max)
            row_sum = jnp.sum(expo, axis=-1, keepdims=True)
            probs = (expo / row_sum).astype(jnp.bfloat16)
            mixed = jnp.einsum("hqk,khd->qhd", probs, values, preferred_element_type=jnp.float32)
            return (mixed.astype(jnp.bfloat16), row_max[..., 0] + jnp.log(row_sum[..., 0]))

        mixed_blocks, log_sums = lax.map(attend, query_blocks)
        mixed_heads = mixed_blocks.reshape(seq_len, heads_dev * HEAD)
        attn_branch = lax.psum_scatter(
            jnp.dot(mixed_heads, out_weight, preferred_element_type=jnp.float32).astype(
                jnp.bfloat16
            ),
            "mp",
            scatter_dimension=0,
            tiled=True,
        ).astype(jnp.float32)
        resid = inputs_f + attn_branch
        norm_b = normed(resid, norm_gains[1], scale_b)
        hidden_b = lax.all_gather(norm_b.astype(jnp.bfloat16), "mp", axis=0, tiled=True)
        up_proj = jnp.dot(hidden_b, up_weight, preferred_element_type=jnp.float32)
        activated = exact_gelu(up_proj).astype(jnp.bfloat16)
        mlp_branch = lax.psum_scatter(
            jnp.dot(activated, down_weight, preferred_element_type=jnp.float32).astype(
                jnp.bfloat16
            ),
            "mp",
            scatter_dimension=0,
            tiled=True,
        ).astype(jnp.float32)
        layer_out = (resid + mlp_branch).astype(jnp.bfloat16)
        cot_all = lax.all_gather(cot_rows, "mp", axis=0, tiled=True)
        d_act = jnp.einsum("td,fd->tf", cot_all, down_weight, preferred_element_type=jnp.float32)
        grad_down = jnp.einsum("tf,td->fd", activated, cot_all, preferred_element_type=jnp.float32)
        gelu_out, gelu_pull = jax.vjp(exact_gelu, up_proj)
        d_up = gelu_pull(d_act)[0].astype(jnp.bfloat16)
        grad_up = jnp.einsum("td,tf->df", hidden_b, d_up, preferred_element_type=jnp.float32)
        d_norm_b = lax.psum_scatter(
            jnp.einsum("tf,df->td", d_up, up_weight, preferred_element_type=jnp.float32).astype(
                jnp.bfloat16
            ),
            "mp",
            scatter_dimension=0,
            tiled=True,
        ).astype(jnp.float32)
        norm_out_b, norm_pull_b = jax.vjp(normed, resid, norm_gains[1], scale_b)
        d_resid_ln, d_gain_b, d_scale_b = norm_pull_b(d_norm_b)
        d_resid = cot_rows.astype(jnp.float32) + d_resid_ln
        d_branch = lax.all_gather(d_resid.astype(jnp.bfloat16), "mp", axis=0, tiled=True)
        d_mixed = jnp.einsum(
            "td,ed->te", d_branch, out_weight, preferred_element_type=jnp.float32
        ).astype(jnp.bfloat16)
        grad_out = jnp.einsum(
            "te,td->ed", mixed_heads, d_branch, preferred_element_type=jnp.float32
        )
        d_mixed_blocks = d_mixed.reshape(block_count, block_rows, heads_dev, HEAD)

        def attend_back(sums, block_in):
            query_block, d_mix_block, log_block = block_in
            scores = masked_scores(query_block, key_rows, key_valid)
            probs_f = jnp.exp(scores - log_block[..., None])
            d_probs = jnp.einsum(
                "qhd,khd->hqk", d_mix_block, values, preferred_element_type=jnp.float32
            )
            inner = jnp.sum(probs_f * d_probs, axis=-1, keepdims=True)
            d_raw = (probs_f * (d_probs - inner) * 0.125).astype(jnp.bfloat16)
            d_query = jnp.einsum(
                "hqk,khd->qhd", d_raw, key_rows, preferred_element_type=jnp.float32
            )
            d_key = sums[0] + jnp.einsum(
                "hqk,qhd->khd", d_raw, query_block, preferred_element_type=jnp.float32
            )
            d_value = sums[1] + jnp.einsum(
                "hqk,qhd->khd",
                probs_f.astype(jnp.bfloat16),
                d_mix_block,
                preferred_element_type=jnp.float32,
            )
            return ((d_key, d_value), d_query)

        zero_keys = jnp.zeros((seq_len, heads_dev, HEAD), jnp.float32)
        kv_sums, d_query_blocks = lax.scan(
            attend_back, (zero_keys, zero_keys), (query_blocks, d_mixed_blocks, log_sums)
        )
        d_qkv = jnp.stack(
            [
                d_query_blocks.reshape(seq_len, heads_dev * HEAD),
                kv_sums[0].reshape(seq_len, heads_dev * HEAD),
                kv_sums[1].reshape(seq_len, heads_dev * HEAD),
            ]
        ).astype(jnp.bfloat16)
        grad_qkv = jnp.einsum("td,cte->cde", hidden_a, d_qkv, preferred_element_type=jnp.float32)
        d_norm_a = lax.psum_scatter(
            jnp.einsum("cte,cde->td", d_qkv, qkv_weight, preferred_element_type=jnp.float32).astype(
                jnp.bfloat16
            ),
            "mp",
            scatter_dimension=0,
            tiled=True,
        ).astype(jnp.float32)
        norm_out_a, norm_pull_a = jax.vjp(normed, inputs_f, norm_gains[0], scale_a)
        d_input_ln, d_gain_a, d_scale_a = norm_pull_a(d_norm_a)
        input_grad = (d_resid + d_input_ln).astype(jnp.bfloat16)
        weight_terms = (grad_qkv, grad_out, grad_up, grad_down)
        new_weights = jax.tree.map(lambda held, fresh: held + fresh, totals[0], weight_terms)
        new_gains = totals[1] + jnp.stack([d_gain_a, d_gain_b])
        d_pair = jnp.concatenate([d_scale_a, d_scale_b])
        return ((new_weights, new_gains), (layer_out, input_grad, d_pair))

    start_weights = (
        jnp.zeros(qkv_weight.shape, jnp.float32),
        jnp.zeros(out_weight.shape, jnp.float32),
        jnp.zeros(up_weight.shape, jnp.float32),
        jnp.zeros(down_weight.shape, jnp.float32),
    )
    start_gains = jnp.zeros(norm_gains.shape, jnp.float32)
    final_totals, per_item = lax.scan(
        step_item, (start_weights, start_gains), (token_items, cot_items, len_items, pairs)
    )
    weight_totals, gain_totals = final_totals
    layer_outs, input_grads, d_pairs = per_item
    weight_totals = (
        lax.psum_scatter(
            weight_totals[0].astype(jnp.bfloat16), "dp", scatter_dimension=1, tiled=True
        ).astype(jnp.float32),
        lax.psum_scatter(
            weight_totals[1].astype(jnp.bfloat16), "dp", scatter_dimension=1, tiled=True
        ).astype(jnp.float32),
        lax.psum_scatter(
            weight_totals[2].astype(jnp.bfloat16), "dp", scatter_dimension=0, tiled=True
        ).astype(jnp.float32),
        lax.psum_scatter(
            weight_totals[3].astype(jnp.bfloat16), "dp", scatter_dimension=1, tiled=True
        ).astype(jnp.float32),
    )
    time_part = jnp.dot(feats.T, d_pairs, precision=lax.Precision.HIGHEST)
    gains_grad, time_grad = (
        lax.psum_scatter(gain_totals, ("dp", "mp"), scatter_dimension=1, tiled=True),
        lax.psum_scatter(time_part, ("dp", "mp"), scatter_dimension=1, tiled=True),
    )
    return (
        layer_outs.reshape(tokens.shape),
        input_grads.reshape(tokens.shape),
        weight_totals[0],
        weight_totals[1],
        weight_totals[2],
        weight_totals[3],
        gains_grad,
        time_grad,
    )


BF = jnp.bfloat16
F32 = jnp.float32
VMEM_LIMIT = 62 << 20
EXP_SCALE = 0.125 * math.log2(math.e)
HOLD = pl.Buffered(1)
ANY = pl.BlockSpec(memory_space=pl.ANY)


def contract(left, right, left_dim, right_dim):
    return lax.dot_general(
        left, right, (((left_dim,), (right_dim,)), ((), ())), preferred_element_type=F32
    )


def call(
    body, meta, args, grid, in_specs, out_specs, out_shape, flops, scratch=(), aliases=None, weight=0.5
):
    moved = sum(a.size * a.dtype.itemsize for a in args)
    moved += sum(math.prod(o.shape) * jnp.dtype(o.dtype).itemsize for o in out_shape)
    return pl.pallas_call(
        body,
        grid_spec=pltpu.PrefetchScalarGridSpec(
            num_scalar_prefetch=1,
            grid=grid,
            in_specs=in_specs,
            out_specs=out_specs,
            scratch_shapes=list(scratch),
        ),
        out_shape=out_shape,
        input_output_aliases=aliases or {},
        compiler_params=pltpu.CompilerParams(vmem_limit_bytes=VMEM_LIMIT),
        cost_estimate=pl.CostEstimate(
            flops=int(flops * weight), bytes_accessed=int(moved * 0.01), transcendentals=0
        ),
    )(meta, *args)


def shape(dims, kind=BF):
    return jax.ShapeDtypeStruct(tuple(dims), kind)


def normalize(values):
    center = values - jnp.mean(values, axis=-1, keepdims=True)
    spread = jnp.mean(center * center, axis=-1, keepdims=True)
    root = lax.rsqrt(spread + 1e-05)
    return center * root, root


def norm_back(d_out, unit, root, gain):
    d_unit = d_out * gain
    return root * (
        d_unit
        - jnp.mean(d_unit, axis=-1, keepdims=True)
        - unit * jnp.mean(d_unit * unit, axis=-1, keepdims=True)
    )


def first_proj(meta, s, tok, recv, gain, weight, prev):
    _, rows, width = tok.shape
    part = weight.shape[2]
    seqs = gain.shape[0]

    def body(m, loc, rec, g, w, *refs):
        tokf, hid, qkv = refs[-3:]

        @pl.when(pl.program_id(0) == m[0])
        def _():
            tokf[0] = loc[0]

        @pl.when(pl.program_id(0) != m[0])
        def _():
            tokf[0] = rec[0]

        unit, _ = normalize(tokf[0].astype(F32))
        hidden = (unit * g[0]).astype(BF)
        hid[0] = hidden
        for c in range(3):
            qkv[0, c] = contract(w[c], hidden, 0, 1).astype(BF)

    length = 2 * rows
    outs = [shape((seqs, length, width)), shape((seqs, length, width)), shape((seqs, 3, part, length))]
    return call(
        body,
        meta,
        [tok, recv, gain, weight] + list(prev),
        (2,),
        [
            pl.BlockSpec((1, rows, width), lambda h, m: (m[1 + s], 0, 0)),
            pl.BlockSpec((1, rows, width), lambda h, m: (0, 0, 0)),
            pl.BlockSpec((1, 1, width), lambda h, m: (s, 0, 0)),
            pl.BlockSpec((3, width, part), lambda h, m: (0, 0, 0), pipeline_mode=HOLD),
        ]
        + [ANY] * len(prev),
        [
            pl.BlockSpec((1, rows, width), lambda h, m: (s, h, 0)),
            pl.BlockSpec((1, rows, width), lambda h, m: (s, h, 0)),
            pl.BlockSpec((1, 3, part, rows), lambda h, m: (s, 0, 0, h)),
        ],
        outs,
        6 * length * width * part,
        weight=0.8,
        aliases={5 + i: i for i in range(len(prev))},
    )


def other_proj(meta, hid, weight, s, prev):
    seqs, length, width = hid.shape
    part = weight.shape[2]
    rows = length // 2

    def body(m, h_ref, w, *refs):
        for c in range(3):
            refs[-1][0, c] = contract(w[c], h_ref[0], 0, 1).astype(BF)

    return call(
        body,
        meta,
        [hid, weight] + list(prev),
        (2,),
        [
            pl.BlockSpec((1, rows, width), lambda h, m: (s, h, 0)),
            pl.BlockSpec((3, width, part), lambda h, m: (0, 0, 0), pipeline_mode=HOLD),
        ]
        + [ANY] * len(prev),
        [pl.BlockSpec((1, 3, part, rows), lambda h, m: (s, 0, 0, h))],
        [shape((seqs, 3, part, length))],
        6 * length * width * part,
        weight=0.8,
        aliases={3 + i: i for i in range(len(prev))},
    )


def mask_rows(valid, extent, block):
    first = lax.broadcasted_iota(jnp.int32, (16, extent), 0) == 0
    hidden = lax.broadcasted_iota(jnp.int32, (16, extent), 1) >= valid
    keys = jnp.where(first & hidden, -1e30, 0.0).astype(BF)
    ones = jnp.where(lax.broadcasted_iota(jnp.int32, (16, block), 0) == 0, 1.0, 0.0).astype(BF)
    return keys, ones


def by_extent(valid, length, work):
    step = min(256, length)
    for extent in range(step, length + 1, step):
        low = extent - step if extent > step else -1
        high = extent if extent < length else length * 2

        @pl.when((valid > low) & (valid <= high))
        def _():
            work(extent)


def attention(meta, qkv, first, count, prev):
    seqs, _, part, length = qkv.shape
    heads = part // HEAD
    view = qkv.reshape(seqs, 3, heads, HEAD, length)
    lens_at = 1 + seqs

    def body(m, q, k, v, *refs):
        out, logs = refs[-2:]
        valid = m[lens_at + first + pl.program_id(0)]

        def work(extent):
            key_mask, ones = mask_rows(valid, extent, length)
            keys = jnp.concatenate([k[0, 0, 0, :, :extent], key_mask], 0)
            scores = contract(keys, jnp.concatenate([q[0, 0, 0], ones], 0), 0, 0)
            top = jnp.max(scores, 0, keepdims=True)
            expo = jnp.exp2((scores - top) * EXP_SCALE)
            total = jnp.sum(expo, 0, keepdims=True)
            mixed = contract(v[0, 0, 0, :, :extent], expo.astype(BF), 1, 0)
            out[0, 0] = (mixed / total).astype(BF)
            logs[0, 0] = top * EXP_SCALE + jnp.log2(total)

        by_extent(valid, length, work)

    def spec(c):
        return pl.BlockSpec((1, 1, 1, HEAD, length), lambda s, h, m: (s + first, c, h, 0, 0))

    return call(
        body,
        meta,
        [view, view, view] + list(prev),
        (count, heads),
        [spec(0), spec(1), spec(2)] + [ANY] * len(prev),
        [
            pl.BlockSpec((1, 1, HEAD, length), lambda s, h, m: (s + first, h, 0, 0)),
            pl.BlockSpec((1, 1, 1, length), lambda s, h, m: (s + first, h, 0, 0)),
        ],
        [shape((seqs, heads, HEAD, length)), shape((seqs, heads, 1, length), F32)],
        16 * count * heads * length * length * HEAD,
        aliases={4 + i: i for i in range(len(prev))},
    )


def attention_back(meta, qkv, out, d_out, logs, first, prev):
    seqs, _, part, length = qkv.shape
    heads = part // HEAD
    view = qkv.reshape(seqs, 3, heads, HEAD, length)
    lens_at = 1 + seqs
    block = min(256, length)
    group = 2 if heads % 2 == 0 else 1

    def body(m, q, k, v, o, do, ls, *refs):
        d_qkv, dk_sum, dv_sum = refs[-3:]
        valid = m[lens_at + first]

        def work(extent):
            key_mask, ones = mask_rows(valid, extent, block)
            for h in range(group):
                keys = k[0, 0, h, :, :extent]
                vals = v[0, 0, h, :, :extent]
                masked_keys = jnp.concatenate([keys, key_mask], 0)
                for i in range(length // block):
                    sl = slice(i * block, (i + 1) * block)
                    query = q[0, 0, h, :, sl]
                    d_mix = do[0, h, :, sl]
                    scores = contract(masked_keys, jnp.concatenate([query, ones], 0), 0, 0)
                    probs = jnp.exp2(scores * EXP_SCALE - ls[0, h, :, sl])
                    inner = jnp.sum(d_mix.astype(F32) * o[0, h, :, sl].astype(F32), 0, keepdims=True)
                    d_probs = contract(vals, d_mix, 0, 0)
                    d_raw = (probs * (d_probs - inner) * 0.125).astype(BF)
                    d_value = contract(d_mix, probs.astype(BF), 1, 1)
                    d_key = contract(query, d_raw, 1, 1)
                    if i == 0:
                        dk_sum[:, :extent] = d_key
                        dv_sum[:, :extent] = d_value
                    else:
                        dk_sum[:, :extent] += d_key
                        dv_sum[:, :extent] += d_value
                    d_qkv[0, 0, h, :, sl] = contract(keys, d_raw, 1, 0).astype(BF)
                d_qkv[0, 1, h, :, :extent] = dk_sum[:, :extent].astype(BF)
                d_qkv[0, 2, h, :, :extent] = dv_sum[:, :extent].astype(BF)
                if extent < length:
                    rest = jnp.zeros((HEAD, length - extent), BF)
                    d_qkv[0, 1, h, :, extent:] = rest
                    d_qkv[0, 2, h, :, extent:] = rest

        by_extent(valid, length, work)

    def spec(c):
        return pl.BlockSpec((1, 1, group, HEAD, length), lambda h, m: (first, c, h, 0, 0))

    head_spec = pl.BlockSpec((1, group, HEAD, length), lambda h, m: (first, h, 0, 0))
    return call(
        body,
        meta,
        [view, view, view, out, d_out, logs] + list(prev),
        (heads // group,),
        [
            spec(0),
            spec(1),
            spec(2),
            head_spec,
            head_spec,
            pl.BlockSpec((1, group, 1, length), lambda h, m: (first, h, 0, 0)),
        ]
        + [ANY] * len(prev),
        [pl.BlockSpec((1, 3, group, HEAD, length), lambda h, m: (first, 0, h, 0, 0))],
        [shape((seqs, 3, heads, HEAD, length))],
        40 * heads * length * length * HEAD,
        weight=0.02,
        scratch=[pltpu.VMEM((HEAD, length), F32)] * 2,
        aliases={7 + i: i for i in range(len(prev))},
    )


def out_proj(meta, own_mix, oth_mix, tokf, own_w, oth_w, gain):
    seqs, length, width = tokf.shape
    rows = length // 2
    part = own_w.shape[0]
    own_mix = own_mix.reshape(seqs, part, length)
    oth_mix = oth_mix.reshape(seqs, part, length)

    def body(m, a, b, t, wa, wb, g, resid, hid):
        branch = contract(a[0], wa[...], 0, 0) + contract(b[0], wb[...], 0, 0)
        total = t[0].astype(F32) + branch
        resid[0] = total.astype(BF)
        unit, _ = normalize(total)
        hid[0] = (unit * g[0]).astype(BF)

    mix_spec = pl.BlockSpec((1, part, rows), lambda s, h, m: (s, 0, h))
    row_spec = pl.BlockSpec((1, rows, width), lambda s, h, m: (s, h, 0))
    w_spec = pl.BlockSpec((part, width), lambda s, h, m: (0, 0), pipeline_mode=HOLD)
    return call(
        body,
        meta,
        [own_mix, oth_mix, tokf, own_w, oth_w, gain],
        (seqs, 2),
        [
            mix_spec,
            mix_spec,
            row_spec,
            w_spec,
            w_spec,
            pl.BlockSpec((1, 1, width), lambda s, h, m: (s, 0, 0)),
        ],
        [row_spec] * 2,
        [shape((seqs, length, width))] * 2,
        4 * seqs * length * width * part,
    )


def feed_forward(meta, hid, cot, cot_recv, up_w, down_w):
    seqs, length, width = hid.shape
    tokens = seqs * length
    hidden = up_w.shape[1]
    block = min(512, hidden)
    rows = min(1024, tokens)
    steps = hidden // block
    half_root = 1.0 / math.sqrt(2.0)
    density = 1.0 / math.sqrt(2.0 * math.pi)

    def body(m, h_ref, stay, came, wu, wd, out, d_hid, grads, act, d_up, out_sum, hid_sum, c_ref, stage, sem):
        step = pl.program_id(0)

        def loads():
            moves = []
            for s in range(seqs):
                for k, src in enumerate((stay.at[m[1 + s]], came.at[s])):
                    half = m[0] if k == 0 else 1 - m[0]
                    at = pl.multiple_of(s * length + half * (length // 2), length // 2)
                    dst = c_ref.at[pl.ds(at, length // 2)]
                    moves.append(pltpu.make_async_copy(src, dst, sem.at[s, k]))
            return moves

        def stores():
            return [
                pltpu.make_async_copy(stage.at[0], out, sem.at[seqs, 0]),
                pltpu.make_async_copy(stage.at[1], d_hid, sem.at[seqs, 1]),
            ]

        @pl.when(step == 0)
        def _():
            for move in loads():
                move.start()
            out_sum[...] = jnp.zeros_like(out_sum)
            hid_sum[...] = jnp.zeros_like(hid_sum)
            for move in loads():
                move.wait()

        for r in range(tokens // rows):
            sl = slice(r * rows, (r + 1) * rows)
            up = contract(h_ref[sl, :], wu[...], 1, 0)
            d_act = contract(c_ref[sl, :], wd[...], 1, 1)
            cdf = 0.5 * (1.0 + lax.erf(up * half_root))
            slope = cdf + up * (density * jnp.exp(-0.5 * up * up))
            a = (up * cdf).astype(BF)
            d = (d_act * slope).astype(BF)
            act[sl, :] = a
            d_up[sl, :] = d
            out_sum[sl, :] += contract(a, wd[...], 1, 0)
            hid_sum[sl, :] += contract(d, wu[...], 1, 1)

        @pl.when(step == steps - 1)
        def _():
            stage[0] = out_sum[...].astype(BF)
            stage[1] = hid_sum[...].astype(BF)
            for move in stores():
                move.start()

        grads[0] = contract(h_ref[...], d_up[...], 0, 0).astype(BF)
        grads[1] = contract(c_ref[...], act[...], 0, 0).astype(BF)

        @pl.when(step == steps - 1)
        def _():
            for move in stores():
                move.wait()

    return call(
        body,
        meta,
        [hid.reshape(tokens, width), cot, cot_recv, up_w, down_w],
        (steps,),
        [
            pl.BlockSpec((tokens, width), lambda j, m: (0, 0), pipeline_mode=HOLD),
            ANY,
            ANY,
            pl.BlockSpec((width, block), lambda j, m: (0, j)),
            pl.BlockSpec((block, width), lambda j, m: (j, 0)),
        ],
        [ANY, ANY, pl.BlockSpec((2, width, block), lambda j, m: (0, 0, j))],
        [shape((tokens, width)), shape((tokens, width)), shape((2, width, hidden))],
        12 * tokens * width * hidden,
        weight=0.4,
        scratch=[
            pltpu.VMEM((tokens, block), BF),
            pltpu.VMEM((tokens, block), BF),
            pltpu.VMEM((tokens, width), F32),
            pltpu.VMEM((tokens, width), F32),
            pltpu.VMEM((tokens, width), BF),
            pltpu.VMEM((2, tokens, width), BF),
            pltpu.SemaphoreType.DMA((seqs + 1, 2)),
        ],
    )


def middle(meta, resid, mlp, d_hid, cot, cot_recv, own_mix, oth_mix, own_w, oth_w, gain):
    items = cot.shape[0]
    seqs, length, width = resid.shape
    rows = length // 2
    part = own_w.shape[0]
    mixes = [a.reshape(seqs, part, length) for a in (own_mix, oth_mix)]
    parts = [a.reshape(resid.shape) for a in mlp + d_hid]

    def body(
        m, res, up, up2, dh, dh2, cl, cr, ma, mb, wa, wb, g, mine, away, branch, dma, dmb, grad, gsum, grad_sum, vec, ct
    ):
        phase, s = pl.program_id(0), pl.program_id(1)

        @pl.when((phase == 0) & (s == 0))
        def _():
            grad_sum[...] = jnp.zeros_like(grad_sum)
            vec[...] = jnp.zeros_like(vec)

        resid_f = res[0].astype(F32)
        total = (resid_f + (up[0].astype(F32) + up2[0].astype(F32))).astype(BF)

        @pl.when(phase == 0)
        def _():
            away[0] = total
            ct[...] = cr[0]

        @pl.when(phase == 1)
        def _():
            mine[0] = total
            ct[...] = cl[0]

        unit, root = normalize(resid_f)
        d_out = dh[0].astype(F32) + dh2[0].astype(F32)
        vec[s] += jnp.sum(d_out * unit, axis=0, keepdims=True)
        d_res = (ct[...].astype(F32) + norm_back(d_out, unit, root, g[0])).astype(BF)
        branch[0] = d_res
        dma[0] = contract(wa[...], d_res, 1, 1).astype(BF)
        dmb[0] = contract(wb[...], d_res, 1, 1).astype(BF)
        grad_sum[0] += contract(d_res, ma[0], 0, 1)
        grad_sum[1] += contract(d_res, mb[0], 0, 1)

        @pl.when((phase == 1) & (s == seqs - 1))
        def _():
            grad[...] = grad_sum[...].astype(BF)
            gsum[...] = vec[...]

    def at(p, m):
        return (1 - m[0]) + p * (2 * m[0] - 1)

    row_spec = pl.BlockSpec((1, rows, width), lambda p, s, m: (s, at(p, m), 0))
    mix_spec = pl.BlockSpec((1, part, rows), lambda p, s, m: (s, 0, at(p, m)))
    w_spec = pl.BlockSpec((part, width), lambda p, s, m: (0, 0), pipeline_mode=HOLD)
    return call(
        body,
        meta,
        [resid] + parts + [cot, cot_recv, mixes[0], mixes[1], own_w, oth_w, gain],
        (2, seqs),
        [row_spec] * 5
        + [
            pl.BlockSpec((1, rows, width), lambda p, s, m: (m[1 + p * s], 0, 0)),
            pl.BlockSpec((1, rows, width), lambda p, s, m: (s + p * (seqs - 1 - s), 0, 0)),
        ]
        + [mix_spec] * 2
        + [w_spec] * 2
        + [pl.BlockSpec((1, 1, width), lambda p, s, m: (s, 0, 0))],
        [
            pl.BlockSpec((1, rows, width), lambda p, s, m: (m[1 + p * s], 0, 0)),
            pl.BlockSpec((1, rows, width), lambda p, s, m: (s + p * (seqs - 1 - s), 0, 0)),
            row_spec,
            mix_spec,
            mix_spec,
            pl.BlockSpec((2, width, part), lambda p, s, m: (0, 0, 0), pipeline_mode=HOLD),
            pl.BlockSpec((seqs, 1, width), lambda p, s, m: (0, 0, 0)),
        ],
        [
            shape((items, rows, width)),
            shape((seqs, rows, width)),
            shape((seqs, length, width)),
            shape((seqs, part, length)),
            shape((seqs, part, length)),
            shape((2, width, part)),
            shape((seqs, 1, width), F32),
        ],
        8 * seqs * length * width * part,
        weight=1.0,
        scratch=[
            pltpu.VMEM((2, width, part), F32),
            pltpu.VMEM((seqs, 1, width), F32),
            pltpu.VMEM((rows, width), BF),
        ],
    )


def proj_grad(meta, hid, d_qkv, dp_count):
    seqs, length, width = hid.shape
    part = d_qkv.shape[2] * d_qkv.shape[3]
    d_qkv = d_qkv.reshape(seqs, 3, part, length)
    per = width // dp_count
    parity_at = 1 + 3 * seqs

    def body(m, h_ref, d_ref, keep, send):
        total = contract(d_ref[0, 0], h_ref[0], 1, 0)
        for s in range(1, seqs):
            total += contract(d_ref[s, 0], h_ref[s], 1, 0)
        grad = total.astype(BF).T.reshape(dp_count // 2, 2, per, part)
        even = grad[:, 0].reshape(width // 2, part)
        odd = grad[:, 1].reshape(width // 2, part)

        @pl.when(m[parity_at] == 0)
        def _():
            keep[0] = even
            send[0] = odd

        @pl.when(m[parity_at] != 0)
        def _():
            keep[0] = odd
            send[0] = even

    return call(
        body,
        meta,
        [hid, d_qkv],
        (3,),
        [
            pl.BlockSpec((seqs, length, width), lambda c, m: (0, 0, 0), pipeline_mode=HOLD),
            pl.BlockSpec((seqs, 1, part, length), lambda c, m: (0, c, 0, 0)),
        ],
        [pl.BlockSpec((1, width // 2, part), lambda c, m: (c, 0, 0))] * 2,
        [shape((3, width // 2, part))] * 2,
        6 * seqs * length * width * part,
        weight=0.02,
    )


def input_back(meta, tokf, branch, own_d, oth_d, own_w, oth_w, gain, items, stay, s, prev):
    seqs, length, width = tokf.shape
    rows = length // 2
    part = own_w.shape[2]
    block = min(256, rows)
    cuts = rows // block
    own_d = own_d.reshape(seqs, 3, part, length)
    oth_d = oth_d.reshape(seqs, 3, part, length)

    def body(m, tok, br, da, db, wa, wb, g, *refs):
        out, gsum = refs[-2:]
        d_hid = contract(da[0, 0], wa[0], 0, 1) + contract(db[0, 0], wb[0], 0, 1)
        for c in range(1, 3):
            d_hid += contract(da[0, c], wa[c], 0, 1) + contract(db[0, c], wb[c], 0, 1)
        unit, root = normalize(tok[0].astype(F32))
        vec = jnp.sum(d_hid * unit, axis=0, keepdims=True)

        @pl.when(pl.program_id(0) == 0)
        def _():
            gsum[0] = vec

        @pl.when(pl.program_id(0) > 0)
        def _():
            gsum[0] += vec

        out[0] = (br[0].astype(F32) + norm_back(d_hid, unit, root, g[0])).astype(BF)

    def at(i, m):
        return (m[0] if stay else 1 - m[0]) * cuts + i

    row_spec = pl.BlockSpec((1, block, width), lambda i, m: (s, at(i, m), 0))
    d_spec = pl.BlockSpec((1, 3, part, block), lambda i, m: (s, 0, 0, at(i, m)))
    w_spec = pl.BlockSpec((3, width, part), lambda i, m: (0, 0, 0), pipeline_mode=HOLD)
    return call(
        body,
        meta,
        [tokf, branch, own_d, oth_d, own_w, oth_w, gain] + list(prev),
        (cuts,),
        [row_spec, row_spec, d_spec, d_spec, w_spec, w_spec]
        + [pl.BlockSpec((1, 1, width), lambda i, m: (s, 0, 0))]
        + [ANY] * len(prev),
        [
            pl.BlockSpec((1, block, width), lambda i, m: (m[1 + s] if stay else 0, i, 0)),
            pl.BlockSpec((1, 1, width), lambda i, m: (0, 0, 0)),
        ],
        [shape((items if stay else 1, rows, width)), shape((1, 1, width), F32)],
        12 * rows * width * part,
        weight=0.02,
        aliases={8 + i: i for i in range(len(prev))},
    )


def place(meta, bases, came):
    seqs, at = len(came[0]), 1 + 2 * len(came[0])
    _, rows, width = bases[0].shape
    flat = [moved for group in came for moved in group]

    def body(m, *refs):
        outs = refs[len(flat) + len(bases) :]
        for s in range(seqs):

            @pl.when(pl.program_id(0) == s)
            def _():
                for g in range(len(bases)):
                    outs[g][...] = refs[g * seqs + s][...]

    return call(
        body,
        meta,
        flat + list(bases),
        (seqs,),
        [pl.BlockSpec((1, rows, width), lambda s, m: (0, 0, 0), pipeline_mode=HOLD)] * len(flat)
        + [ANY] * len(bases),
        [pl.BlockSpec((1, rows, width), lambda s, m: (m[at + s], 0, 0))] * len(bases),
        [shape(b.shape) for b in bases],
        1,
        aliases={1 + len(flat) + i: i for i in range(len(bases))},
    )


def after(value, *earlier):
    return lax.optimization_barrier((value,) + earlier)[0]


def per_device_pair(
    tokens,
    lengths,
    timesteps,
    norm_gains,
    time_weight,
    qkv_weight,
    out_weight,
    up_weight,
    down_weight,
    cotangent,
):
    micro_count, seq_dev, rows, width = tokens.shape
    items = micro_count * seq_dev
    seqs = items // 2
    x = lax.axis_index("mp")
    dp = lax.axis_index("dp")
    dp_count = lax.axis_size("dp")
    part = qkv_weight.shape[2]
    hidden = up_weight.shape[1]
    tok = tokens.reshape(items, rows, width)
    cot = cotangent.reshape(items, rows, width)
    lens = lengths.reshape(items)
    steps = timesteps.reshape(items)

    at = jnp.arange(items, dtype=jnp.int32)
    longer = (lens[None, :] > lens[:, None]) | (
        (lens[None, :] == lens[:, None]) & (at[None, :] < at[:, None])
    )
    rank = jnp.sum(longer.astype(jnp.int32), axis=1)
    holder = (rank + 1) // 2 % 2
    slot = rank // 2

    def chosen(device, values):
        hit = (holder == device)[None, :] & (slot[None, :] == jnp.arange(seqs)[:, None])
        return jnp.sum(jnp.where(hit, values[None, :], 0), axis=1)

    own, oth = chosen(x, at), chosen(1 - x, at)
    meta = jnp.concatenate([x[None], own, chosen(x, lens), oth, dp[None] % 2]).astype(jnp.int32)

    def swap(value):
        return lax.ppermute(value, "mp", [(0, 1), (1, 0)])

    def shard(value):
        count = value.shape[0] // dp_count
        return lax.dynamic_slice_in_dim(value, dp * count, count, 0)

    def spread(value):
        return lax.all_gather(value, "dp", axis=0, tiled=True)

    qkv_rows = qkv_weight.reshape(3 * width, part)
    def sent(rows_of, s):
        return lax.dynamic_slice_in_dim(rows_of, oth[s], 1, 0)

    tok_first = sent(tok, 0)
    tok_recv = [swap(tok_first)]
    qkv_shard = swap(after(shard(qkv_rows), tok_first))
    qkv_oth = spread(qkv_shard).reshape(qkv_weight.shape)

    feats = sinusoid(chosen(x, steps))
    pairs = jnp.dot(feats, time_weight, precision=lax.Precision.HIGHEST)
    widened = 1.0 + pairs.reshape(seqs, 2, 1, width)
    gain_a = norm_gains[0] * widened[:, 0]
    gain_b = norm_gains[1] * widened[:, 1]

    near = [shard(w).reshape(-1, width) for w in (out_weight, up_weight, down_weight)]
    far = swap(after(jnp.concatenate(near, 0), tok_recv[0]))
    base, qkv_far, mix_own, mix_oth = (), (), (), ()
    for s in range(seqs):
        head = s == 0
        base = first_proj(meta, s, tok, tok_recv[s], gain_a, qkv_weight, base)
        mix_own = attention(meta, base[2], s, 1, mix_own)
        if s + 1 < seqs:
            tok_recv.append(swap(after(sent(tok, s + 1), tok_recv[s])))
        order = after(meta, far) if head else meta
        qkv_far = other_proj(order, base[1], qkv_oth, s, qkv_far)
        if head:
            arrived = after(far, base[2])
            cuts = [0]
            for piece in near:
                cuts.append(cuts[-1] + piece.shape[0])
            out_oth, up_oth, down_oth = [
                spread(arrived[cuts[i] : cuts[i + 1]].reshape(w.shape[0] // dp_count, w.shape[1]))
                for i, w in enumerate((out_weight, up_weight, down_weight))
            ]
        mix_oth = attention(meta, qkv_far[0], s, 1, mix_oth)
        if head:
            cot_sent = jnp.concatenate([sent(cot, i) for i in range(seqs)], 0)
            cot_recv = swap(after(cot_sent, tok_recv[-1]))
    tokf, hid_a, qkv_own = base
    qkv_far = qkv_far[0]
    resid, hid_b = out_proj(meta, mix_own[0], mix_oth[0], tokf, out_weight, out_oth, gain_b)
    mlp_own, back_own, grads_own = feed_forward(meta, hid_b, cot, cot_recv, up_weight, down_weight)
    mlp_oth, back_oth, grads_oth = feed_forward(
        after(meta, grads_own), hid_b, cot, cot_recv, up_oth, down_oth
    )

    def tree_send(value, step):
        count, cols = value.shape[0], value.shape[-1]
        value = value.reshape(count, -1, 1, 2, width // dp_count, cols)
        mine_at = dp // step % 2
        keep = lax.dynamic_index_in_dim(value, mine_at, 3, False)
        send = lax.dynamic_index_in_dim(value, 1 - mine_at, 3, False)
        return keep, lax.ppermute(send, "dp", [(i, i ^ step) for i in range(dp_count)])

    def tree_add(pair, gate):
        keep, came = pair[0], after(pair[1], *gate)
        return (keep.astype(F32) + came.astype(F32)).astype(BF)

    def tree(value):
        step = 1
        if not hasattr(value, "reshape"):
            keep, send = value
            came = lax.ppermute(send, "dp", [(i, i ^ 1) for i in range(dp_count)])
            value = tree_add((keep, came), (yield keep))
            step = 2
        while step * 4 < dp_count:
            pair = tree_send(value, step)
            value = tree_add(pair, (yield value))
            step *= 2
        left = dp_count // step
        held = value
        value = value.reshape(value.shape[0], left, width // dp_count, value.shape[-1])
        place_at = dp // step

        def piece(k):
            return lax.dynamic_index_in_dim(value, place_at ^ k, 1, False)

        came = [
            lax.ppermute(piece(k), "dp", [(i, i ^ (k * step)) for i in range(dp_count)])
            for k in range(1, left)
        ]
        gate = yield held
        total = piece(0).astype(F32)
        for part_in in came:
            total += after(part_in, *gate).astype(F32)
        yield total.astype(BF)

    def reduce(value):
        return lax.psum_scatter(value, "dp", scatter_dimension=1, tiled=True)

    ffn_own = reduce(grads_own)
    ffn_oth = reduce(grads_oth)
    out_stay, out_away, branch, d_mix_own, d_mix_oth, out_grads, sum_b = middle(
        meta,
        resid,
        [mlp_own, mlp_oth],
        [back_own, back_oth],
        cot,
        cot_recv,
        mix_own[0],
        mix_oth[0],
        out_weight,
        out_oth,
        gain_b,
    )
    out_came = []

    def heads_view(value):
        return value.reshape(seqs, part // HEAD, HEAD, 2 * rows)

    class Job:
        def __init__(self, value):
            self.run, self.value, self.done = tree(value), None, False
            self.value = next(self.run)

        def go(self, *gate):
            if not self.done:
                try:
                    self.value = self.run.send(gate)
                except StopIteration:
                    self.done = True
            return self.value

    d_mix_own, d_mix_oth = heads_view(d_mix_own), heads_view(d_mix_oth)
    out_job = Job(out_grads)
    d_oth, d_own = (), ()
    order = meta
    for s in range(seqs):
        d_oth = attention_back(order, qkv_far, mix_oth[0], d_mix_oth, mix_oth[1], s, d_oth)
        order = after(meta, out_job.go(d_oth[0]))
    grad_oth = proj_grad(order, hid_a, d_oth[0], dp_count)
    oth_job = Job(grad_oth)
    order = after(meta, grad_oth[0], ffn_own)
    for s in range(seqs):
        out_came.append(swap(after(out_away[s : s + 1], d_own[0] if s else grad_oth[0])))
        d_own = attention_back(order, qkv_own, mix_own[0], d_mix_own, mix_own[1], s, d_own)
        order = after(meta, oth_job.go(d_own[0]), out_came[s])
        if s == seqs - 1:
            order = after(order, out_job.go(d_own[0]))
    grad_own = proj_grad(order, hid_a, d_own[0], dp_count)
    own_job = Job(grad_own)
    order = after(meta, grad_own[0])
    in_away, in_stay, sum_a = [], (), []

    def last_back(order, s, stay, prev):
        return input_back(
            order, tokf, branch, d_own[0], d_oth[0], qkv_weight, qkv_oth, gain_a, items, stay, s, prev
        )

    for s in range(seqs):
        rows_out, vec = last_back(order, s, False, ())
        in_away.append(swap(rows_out))
        sum_a.append(vec)
        order = after(meta, rows_out, own_job.go(rows_out) if s == 0 else oth_job.go(rows_out))
        if s == 0:
            order = after(order, ffn_oth)
    out_red, qkv_red_oth = out_job.value, oth_job.value
    far_grads = swap(
        jnp.concatenate([ffn_oth[0], ffn_oth[1], out_red[1]] + [qkv_red_oth[c] for c in range(3)], 1)
    )
    for s in range(seqs):
        rows_out, vec = last_back(order, s, True, in_stay)
        in_stay = (rows_out,)
        sum_a[s] += vec
        order = after(meta, own_job.go(rows_out) if s == 0 else rows_out)
    sum_a = jnp.concatenate(sum_a, 0)
    output, input_grad = place(order, [out_stay, in_stay[0]], [out_came, in_away])

    sums = jnp.stack([sum_a, sum_b], 0)[:, :, 0]
    d_pair = sums * norm_gains[:, None, :]
    gain_part = jnp.sum(sums * jnp.swapaxes(widened[:, :, 0], 0, 1), axis=1)
    count = 2 * dp_count
    cols, gain_cols, time_cols = 2 * width // count, width // count, feats.shape[1]
    by_pair = jnp.moveaxis(d_pair.reshape(2, seqs, dp_count, cols), 1, 2).reshape(count, seqs * cols)
    by_gain = jnp.moveaxis(gain_part.reshape(2, count, gain_cols), 0, 1).reshape(count, 2 * gain_cols)
    by_feat = jnp.broadcast_to(feats.reshape(1, seqs * time_cols), (count, seqs * time_cols))
    packed = jnp.concatenate([by_pair, by_gain, by_feat], 1)
    packed = after(packed, *in_away)
    everyone = lax.all_to_all(packed, ("dp", "mp"), 0, 0, tiled=True)
    far_grads = after(far_grads, everyone)
    while not own_job.done:
        own_job.go(everyone)
    everyone = after(everyone, output, input_grad)
    mine = everyone[:, : seqs * cols].reshape(count * seqs, cols)
    gains_grad = jnp.sum(everyone[:, seqs * cols :][:, : 2 * gain_cols], axis=0).reshape(2, gain_cols)
    all_feats = everyone[:, seqs * cols + 2 * gain_cols :].reshape(count * seqs, time_cols)
    time_grad = jnp.dot(all_feats.T, mine, precision=lax.Precision.HIGHEST)
    def joined(near, first, cols):
        return near.astype(F32) + far_grads[:, first : first + cols].astype(F32)

    up_sum = joined(ffn_own[0], 0, hidden)
    down_sum = joined(ffn_own[1], hidden, hidden)
    out_sum = joined(out_red[0], 2 * hidden, part)
    qkv_sum = jnp.stack(
        [joined(own_job.value[c], 2 * hidden + (1 + c) * part, part) for c in range(3)], 0
    )

    return (
        output.reshape(tokens.shape),
        input_grad.reshape(tokens.shape),
        qkv_sum,
        out_sum.T,
        up_sum,
        down_sum.T,
        gains_grad,
        time_grad,
    )


def solution(mesh):
    in_specs = (
        P(None, "dp", "mp", None),
        P(None, "dp"),
        P(None, "dp"),
        P(),
        P(),
        P(None, None, "mp"),
        P("mp", None),
        P(None, "mp"),
        P("mp", None),
        P(None, "dp", "mp", None),
    )
    out_specs = (
        P(None, "dp", "mp", None),
        P(None, "dp", "mp", None),
        P(None, "dp", "mp"),
        P("mp", "dp"),
        P("dp", "mp"),
        P("mp", "dp"),
        P(None, ("dp", "mp")),
        P(None, ("dp", "mp")),
    )
    dp_count = mesh.shape["dp"]
    paired = mesh.shape["mp"] == 2 and dp_count & (dp_count - 1) == 0 and dp_count > 4
    return jax.shard_map(
        per_device_pair if paired else per_device, mesh=mesh, in_specs=in_specs, out_specs=out_specs, check_vma=False
    )
```
